32 devices in a mesh: gx: 8 (over z, core), gy: 4 (over y, x).
Axes of the slice: x: 2, y: 2, z: 4, core: 2. Of those that a mesh axis runs over, the one named last changes fastest.
Arguments:
- features: bfloat16 [32, 64, 32, 128], P(None, 'gx', 'gy'), may hold values from -6 to 6
- occupancy: int32 [8, 4, 16], replicated, may hold values 0 or 1
- weight_one: bfloat16 [32, 3, 3, 3, 32], replicated, may hold values from -0.21875 to 0.21875
- bias_one: float32 [32], replicated, may hold values from -3 to 3
- weight_two: bfloat16 [32, 3, 3, 3, 32], replicated, may hold values from -0.21875 to 0.21875
- bias_two: float32 [32], replicated, may hold values from -3 to 3
- grad_pooled: bfloat16 [32, 32, 16, 64], P(None, 'gx', 'gy'), may hold values from -24 to 24
- pool_choice: int32 [32, 32, 16, 64], P(None, 'gx', 'gy'), may hold values from 0 to 7
Outputs:
- grad_input: bfloat16 [32, 64, 32, 128], P(None, 'gx', 'gy')
- grad_weight_one: float32 [32, 3, 3, 3, 32], replicated
- grad_bias_one: float32 [32], replicated
- grad_weight_two: float32 [32, 3, 3, 3, 32], replicated
- grad_bias_two: float32 [32], replicated
The draws below stay inside these ranges and needn't reach their ends.
All inputs are finite; a program needn't handle non-finite values.
Results may differ from the reference program's by a relative error of at most 0.035.
The reference program's roundings to bfloat16 on the way (of `masked`, `hidden`, `upstream`, `delta_two` and `delta_one`) count: a program that leaves them out, or rounds other values in their place, can miss the bound.
Values may be sent and summed in bfloat16 or wider, within the bound.
A program may use at most 64 MiB of HBM per device.

```python
import math
import jax
import jax.numpy as jnp
from jax import lax

C = 32
NX = 64
NY = 32
NZ = 128


def touch_ends(array, stream_key, least, high):
    place = [jax.random.randint(jax.random.fold_in(stream_key, axis), (), 0, length) for axis, length in enumerate(array.shape)]
    longest = array.shape.index(max(array.shape))
    next_to = place[:longest] + [(place[longest] + 1) % array.shape[longest]] + place[longest + 1:]
    return array.at[tuple(place)].set(least).at[tuple(next_to)].set(high)


def shard_levels(key, extent, shards, least, top_value):
    def one(dim, blocks):
        heights = jax.random.uniform(jax.random.fold_in(jax.random.fold_in(key, 6), dim), (blocks,), jnp.float32, least / len(shards), top_value / len(shards))
        return jnp.repeat(jnp.exp(heights), extent[dim] // blocks).reshape((-1,) + (1,) * (len(extent) - dim - 1))

    gain = one(*shards[0])
    for cut in shards[1:]:
        gain = gain * one(*cut)
    return gain


def noise(own_key, extent, scale, most, split=(), held_as=jnp.bfloat16):
    drawn = scale * jax.random.normal(own_key, extent, jnp.float32)
    if split:
        drawn = drawn * shard_levels(own_key, extent, split, -0.22, 0.18)
    return jnp.clip(drawn, -most, most).astype(held_as)


def setup_inputs(seed: int = 0) -> dict:
    key_of = jax.random.split(jax.random.key(seed), 9)
    return {
        "features": noise(key_of[0], (C, NX, NY, NZ), 1.0, 6.0, ((1, 8), (2, 4))),
        "occupancy": touch_ends((jax.random.randint(key_of[1], (NX // 8, NY // 8, NZ // 8), 0, 4) < 3).astype(jnp.int32), jax.random.fold_in(key_of[1], 1), 0, 1),
        "weight_one": noise(key_of[2], (C, 3, 3, 3, C), (27 * C) ** -0.5, 0.21875),
        "bias_one": noise(key_of[3], (C,), 0.5, 3.0, (), jnp.float32),
        "weight_two": noise(key_of[4], (C, 3, 3, 3, C), (27 * C) ** -0.5, 0.21875),
        "bias_two": noise(key_of[5], (C,), 0.5, 3.0, (), jnp.float32),
        "grad_pooled": noise(key_of[6], (C, NX // 2, NY // 2, NZ // 2), 4.0, 24.0, ((1, 8), (2, 4))),
        "pool_choice": touch_ends(jax.random.randint(key_of[7], (C, NX // 2, NY // 2, NZ // 2), 0, 8), jax.random.fold_in(key_of[7], 1), 0, 7).astype(jnp.int32),
    }


def convolve(inputs, weight):
    kernel = weight.transpose(0, 4, 1, 2, 3)
    result = lax.conv_general_dilated(inputs[None], kernel, (1, 1, 1), [(1, 1), (1, 1), (1, 1)], dimension_numbers=('NCDHW', 'OIDHW', 'NCDHW'), precision=lax.Precision.HIGHEST)
    return result[0]

def expand(field, factor):
    return jnp.repeat(jnp.repeat(jnp.repeat(field, factor, axis=-3), factor, axis=-2), factor, axis=-1)

def reference(features, occupancy, weight_one, bias_one, weight_two, bias_two, grad_pooled, pool_choice):
    mask = expand(occupancy, 8).astype(jnp.float32)
    masked = features.astype(jnp.float32) * mask
    first_f = weight_one.astype(jnp.float32)
    second_f = weight_two.astype(jnp.float32)
    conv_one, pull_one = jax.vjp(convolve, masked, first_f)
    pre_one = conv_one + bias_one[:, None, None, None]
    hidden = (jnp.maximum(pre_one, 0.0) * mask).astype(jnp.bfloat16)
    conv_two, pull_two = jax.vjp(convolve, hidden.astype(jnp.float32), second_f)
    pre_two = conv_two + bias_two[:, None, None, None]
    spread = expand(grad_pooled.astype(jnp.float32), 2)
    chosen = expand(pool_choice, 2)
    xpos = jnp.arange(NX, dtype=jnp.int32)[:, None, None] % 2
    ypos = jnp.arange(NY, dtype=jnp.int32)[None, :, None] % 2
    zpos = jnp.arange(NZ, dtype=jnp.int32)[None, None, :] % 2
    code = 4 * xpos + 2 * ypos + zpos
    upstream = jnp.where(chosen == code[None], spread, 0.0)
    delta_two = (upstream * (pre_two > 0).astype(jnp.float32) * mask).astype(jnp.bfloat16)
    back_one, grad_w_two = pull_two(delta_two.astype(jnp.float32))
    delta_one = (back_one * (pre_one > 0).astype(jnp.float32) * mask).astype(jnp.bfloat16)
    back_input, grad_w_one = pull_one(delta_one.astype(jnp.float32))
    scale = 1.0 / math.sqrt(NX * NY * NZ)
    grad_input = (back_input * mask).astype(jnp.bfloat16)
    grad_b_one = lax.optimization_barrier(jnp.sum(delta_one.astype(jnp.float32), axis=(1, 2, 3))) * scale
    grad_b_two = lax.optimization_barrier(jnp.sum(delta_two.astype(jnp.float32), axis=(1, 2, 3))) * scale
    return (grad_input, grad_w_one * scale, grad_b_one, grad_w_two * scale, grad_b_two)
```

```python
import functools
import math

import jax
import jax.numpy as jnp
from jax import lax
from jax.experimental import pallas as pl
from jax.experimental.pallas import tpu as pltpu
from jax.sharding import PartitionSpec as P

MESH = pl.DeviceIdType.MESH
HALO = 2
SIDES = ((0, -1), (0, 1), (-1, -1), (-1, 1), (1, -1), (1, 1), (-1, 0), (1, 0))
BF = jnp.bfloat16
F32 = jnp.float32


def edge(side, cells, halo):
    if side == 0:
        return 0, cells
    return (0, halo) if side < 0 else (cells - halo, halo)


def landing(side, cells, halo):
    if side == 0:
        return halo
    return halo + cells if side < 0 else 0


def main_kernel(
    nx, ny, cx, cy, depth, chans,
    f_hbm, occ_hbm, w1_hbm, w2_hbm, b1_hbm, b2_hbm, gp_hbm, pc_hbm,
    gin_ref, sum_ref,
    f_ref, occ_ref, wn1_ref, wn2_ref, b1_ref, b2_ref, gp_ref, pc_ref,
    ft, go, pt, wt, mz_ref, w1_ref, w2_ref, w1b_ref, w2b_ref,
    wide_f, wide_k, wide_w, part1, part2, s1, s2, s3, s4, bias_acc, gw_ref,
    gs, r0, q1, q2, tot,
    local_sem, send_sem, recv_sem, sum_send, sum_recv,
):
    gx = lax.axis_index("gx")
    gy = lax.axis_index("gy")
    nz = nx // 2
    core = lax.rem(gx, 2)
    gz = gx // 2
    taps = 27

    def exists(sx, sy):
        ok_x = jnp.logical_and(gx + sx >= 0, gx + sx < nx)
        ok_y = jnp.logical_and(gy + sy >= 0, gy + sy < ny)
        return jnp.logical_and(ok_x, ok_y)

    partner = (gx + 1 - 2 * core, gy)

    def peer_y(k):
        return (gx, lax.rem(gy + k, ny))

    def peer_z(k):
        return (2 * lax.rem(gz + k, nz) + core, gy)

    barrier = pltpu.get_barrier_semaphore()

    def greet(device):
        pl.semaphore_signal(barrier, inc=1, device_id=device, device_id_type=MESH)

    for k in range(1, nz):
        greet(peer_z(k))
    for k in range(1, ny):
        greet(peer_y(k))
    for sx, sy in SIDES:
        if sx:
            @pl.when(exists(sx, sy))
            def _():
                greet((gx + sx, gy + sy))
    beside_x = (gx > 0).astype(jnp.int32) + (gx < nx - 1).astype(jnp.int32)
    beside_y = (gy > 0).astype(jnp.int32) + (gy < ny - 1).astype(jnp.int32)

    local = [
        pltpu.make_async_copy(src, dst, local_sem.at[n])
        for n, (src, dst) in enumerate((
            (f_hbm, f_ref), (occ_hbm, occ_ref), (w1_hbm, wn1_ref), (w2_hbm, wn2_ref),
            (b1_hbm, b1_ref), (b2_hbm, b2_ref), (gp_hbm, gp_ref), (pc_hbm, pc_ref),
        ))
    ]
    for copy in local:
        copy.start()

    gw_ref[...] = jnp.zeros_like(gw_ref)
    bias_acc[...] = jnp.zeros_like(bias_acc)

    mz_ref[...] = jnp.zeros_like(mz_ref)
    local[1].wait()
    bz = occ_ref.shape[2]
    repeat = (
        lax.broadcasted_iota(jnp.int32, (bz, depth), 1) // (depth // bz)
        == lax.broadcasted_iota(jnp.int32, (bz, depth), 0)
    ).astype(BF)
    for bx in range(occ_ref.shape[0]):
        row = occ_ref[bx].astype(F32).astype(BF)
        mz_ref[bx + 1, 1 : 1 + occ_ref.shape[1], :] = jnp.dot(
            row, repeat, preferred_element_type=F32
        )

    def cell_rows(x, y):
        return pl.ds(x * cy + y, chans, stride=cx * cy)

    local[0].wait()
    ft[...] = f_ref[...].astype(F32).reshape(chans * cx * cy, depth)
    for x in range(cx):
        for y in range(cy):
            wide_f[x + HALO, y + HALO] = ft[cell_rows(x, y), :].astype(BF)

    pl.semaphore_wait(barrier, nz - 1 + ny - 1 + beside_x + beside_x * beside_y)

    def copy_of(n, k):
        sx, sy = SIDES[k]
        ref, halo, wx, wy = (
            (wide_f, HALO, cx, cy), (wide_k, 1, cx // 2, cy // 2), (wide_w, 1, cx // 2, cy // 2)
        )[n]
        fx, lx = edge(sx, wx, halo)
        fy, ly = edge(sy, wy, halo)
        tx, ty = landing(sx, wx, halo), landing(sy, wy, halo)
        return pltpu.make_async_remote_copy(
            src_ref=ref.at[halo + fx : halo + fx + lx, halo + fy : halo + fy + ly],
            dst_ref=ref.at[tx : tx + lx, ty : ty + ly],
            send_sem=send_sem.at[n, k],
            recv_sem=recv_sem.at[n, k],
            device_id=(gx + sx, gy + sy),
            device_id_type=MESH,
        )

    def send(n):
        for k, (sx, sy) in enumerate(SIDES):
            @pl.when(exists(sx, sy))
            def _():
                copy_of(n, k).start()

    def arrive(n, along):
        for k, (sx, sy) in enumerate(SIDES):
            if (sy == 0) in along:
                @pl.when(exists(-sx, -sy))
                def _():
                    copy_of(n, k).wait_recv()

    def sent(n):
        for k, (sx, sy) in enumerate(SIDES):
            @pl.when(exists(sx, sy))
            def _():
                copy_of(n, k).wait_send()

    send(0)

    for n, (nat, fwd, bwd) in enumerate(((wn1_ref, w1_ref, w1b_ref), (wn2_ref, w2_ref, w2b_ref))):
        local[2 + n].wait()
        wide = nat[...].astype(F32)
        for b in range(3):
            fwd[b * chans : (b + 1) * chans, :] = jnp.concatenate(
                [wide[a * 9 + b * 3 + c] for a in range(3) for c in range(3)], axis=1
            ).astype(BF)
        rows = wt.shape[0]
        wt[...] = jnp.zeros_like(wt)
        for a in range(3):
            for c in range(3):
                first = (a * 3 + c) * chans
                wt[first : first + chans, 0 : 3 * chans] = jnp.concatenate(
                    [wide[(2 - a) * 9 + (2 - b) * 3 + 2 - c] for b in range(3)], axis=1
                )
        turned = wt[...].T
        bwd[...] = turned[0 : 3 * chans, 0 : 9 * chans].astype(BF)

    half = depth // 2
    px, py = cx // 2, cy // 2
    spread = (
        lax.broadcasted_iota(jnp.int32, (half, depth), 1) // 2
        == lax.broadcasted_iota(jnp.int32, (half, depth), 0)
    ).astype(BF)
    local[6].wait()
    local[7].wait()
    for n, ref in enumerate((gp_ref, pc_ref)):
        for c in range(chans):
            for x in range(px):
                first = (c * px + x) * py
                pt[n, first : first + py, 0:half] = ref[c, x].astype(F32)
        pt[n] = jnp.dot(pt[n, :, 0:half].astype(BF), spread, preferred_element_type=F32)

    def pooled(n, x, y):
        return pt[n, pl.ds(x * py + y, chans, stride=px * py), :]

    for x in range(px):
        for y in range(py):
            wide_k[x + 1, y + 1] = pooled(1, x, y).astype(BF)
    send(1)

    same = lax.broadcasted_iota(jnp.int32, (chans, chans), 0) == lax.broadcasted_iota(
        jnp.int32, (chans, chans), 1
    )
    local[4].wait()
    local[5].wait()
    bias_one, bias_two = [
        jnp.sum(jnp.where(same, ref[...], 0.0), axis=1, keepdims=True) for ref in (b1_ref, b2_ref)
    ]
    lane = lax.broadcasted_iota(jnp.int32, (1, depth), 1)
    not_first = lane != 0
    not_last = lane != depth - 1
    lane_odd = lane % 2

    def flags(x, y):
        brick = gx * (cx // 8) + (x + 8 - HALO) // 8
        return mz_ref[brick, pl.ds(gy * (cy // 8) + (y + 8 - HALO) // 8, 1), :]

    def lanes_of(y, count=1):
        return slice(y * depth, (y + count) * depth)

    def put(stack, x, y, value):
        rounded = value.astype(BF)
        wide = rounded.astype(F32)
        where = lanes_of(y)
        stack[x, 0:chans, where] = jnp.where(not_first, pltpu.roll(wide, 1, 1), 0.0).astype(BF)
        stack[x, chans : 2 * chans, where] = rounded
        stack[x, 2 * chans : 3 * chans, where] = jnp.where(
            not_last, pltpu.roll(wide, depth - 1, 1), 0.0
        ).astype(BF)
        return rounded

    def put_cell(x, y):
        put(s1, x, y, jnp.where(flags(x, y) > 0, wide_f[x, y].astype(F32), 0.0))

    def conv(weight, stack, x, first, count, outs, total):
        rows = stack[pl.ds(x, 3), :, lanes_of(first, count)].reshape(9 * chans, count * depth)
        full = jnp.dot(weight[...], rows, preferred_element_type=F32)
        for t in range(count):
            for b in range(3):
                y = first + t - b
                if 0 <= y < outs:
                    piece = full[b * chans : (b + 1) * chans, lanes_of(t)]
                    total[y] = total[y] + piece if y in total else piece
        return total

    def grad(slot, delta, stack, x, first):
        width = (cy + 2) * depth
        rows = stack[pl.ds(x, 3), :, first * depth : first * depth + width].reshape(9 * chans, width)
        shifted = []
        for b in range(3):
            parts = []
            if b:
                parts.append(jnp.zeros((chans, b * depth), BF))
            parts.append(delta)
            if b < 2:
                parts.append(jnp.zeros((chans, (2 - b) * depth), BF))
            shifted.append(jnp.concatenate(parts, axis=1))
        left = jnp.concatenate(shifted, axis=0)
        gw_ref[slot, :, 0 : 9 * chans] += lax.dot_general(
            left, rows, (((1,), (1,)), ((), ())), preferred_element_type=F32
        )
        bias_acc[slot] += delta.astype(F32)

    part_rows = 3 * chans // 2

    def pack(slot):
        total = jnp.sum(bias_acc[slot], axis=1, keepdims=True)
        gw_ref[slot, 0:chans, 9 * chans :] = jnp.broadcast_to(
            total, (chans, gw_ref.shape[2] - 9 * chans)
        )
        for n in range(2):
            gs[slot, n] = gw_ref[slot, n * part_rows : (n + 1) * part_rows].astype(BF)

    def sum_copies(slot, phase):
        if phase == 0:
            moves = [(gs.at[slot, 1 - core], r0.at[slot], partner)]
        elif phase == 1:
            moves = [(q1.at[slot, gy], q1.at[slot, gy], peer_y(k)) for k in range(1, ny)]
        elif phase == 2:
            moves = [(q2.at[slot, gz], q2.at[slot, gz], peer_z(k)) for k in range(1, nz)]
        else:
            moves = [(tot.at[slot, core], tot.at[slot, core], partner)]
        return [
            pltpu.make_async_remote_copy(
                src_ref=src, dst_ref=dst,
                send_sem=sum_send.at[slot, phase, k], recv_sem=sum_recv.at[slot, phase, k],
                device_id=device, device_id_type=MESH,
            )
            for k, (src, dst, device) in enumerate(moves)
        ]

    def sum_start(slot, phase):
        for copy in sum_copies(slot, phase):
            copy.start()

    def sum_finish(slot, phase):
        for copy in sum_copies(slot, phase):
            copy.wait_recv()
        if phase == 0:
            q1[slot, gy] = (gs[slot, core].astype(F32) + r0[slot].astype(F32)).astype(BF)
        if phase == 1:
            q2[slot, gz] = sum(q1[slot, k].astype(F32) for k in range(ny)).astype(BF)
        if phase == 2:
            tot[slot, core] = sum(q2[slot, k].astype(F32) for k in range(nz)).astype(BF)

    scale = 1.0 / math.sqrt(cx * nx * cy * ny * depth)

    def publish(slot):
        full = jnp.concatenate([tot[slot, 0], tot[slot, 1]], axis=0).astype(F32) * scale
        for b in range(3):
            for a in range(3):
                for c in range(3):
                    first = (a * 3 + c) * chans
                    sum_ref[slot, a * 9 + b * 3 + c] = full[b * chans : (b + 1) * chans, first : first + chans]
        column = full[0:chans, 9 * chans : 10 * chans]
        row = jnp.sum(jnp.where(same, column, 0.0), axis=0, keepdims=True)
        sum_ref[slot, taps] = jnp.broadcast_to(row, (chans, chans))

    for x in range(cx):
        for y in range(cy):
            put_cell(x + HALO, y + HALO)

    def early_one(x):
        total = conv(w1_ref, s1, x, HALO, cy, cy + 2, {})
        for y in range(2, cy):
            hide(x, y, total[y])
        for n, y in enumerate((0, 1, cy, cy + 1)):
            part1[x, n] = total[y]

    def hide(x, y, pre):
        mask = flags(x + 1, y + 1)
        put(s2, x, y, jnp.where(mask > 0, jnp.maximum(pre + bias_one, 0.0), 0.0))

    for x in range(2, cx):
        early_one(x)
    arrive(0, (True,))
    for n in (0, 1, cx + 2, cx + 3):
        for y in range(cy):
            put_cell(n, y + HALO)
    for x in (0, 1, cx, cx + 1):
        early_one(x)

    def early_two(x):
        total = conv(w2_ref, s2, x, 2, cy - 2, cy, {})
        for y in range(cy):
            part2[x, y] = total[y]

    for x in range(cx):
        early_two(x)

    arrive(0, (False,))
    for x in range(cx + 2 * HALO):
        for y in (0, 1, cy + 2, cy + 3):
            put_cell(x, y)

    for x in range(cx + 2):
        total = {y: part1[x, n] for n, y in enumerate((0, 1, cy, cy + 1))}
        conv(w1_ref, s1, x, 0, 2, cy + 2, total)
        conv(w1_ref, s1, x, cy + 2, 2, cy + 2, total)
        for y in (0, 1, cy, cy + 1):
            hide(x, y, total[y])

    def choose(x):
        total = {y: part2[x, y] for y in range(cy)}
        conv(w2_ref, s2, x, 0, 2, cy, total)
        conv(w2_ref, s2, x, cy, 2, cy, total)
        out = []
        for y in range(cy):
            mask = flags(x + HALO, y + HALO)
            code = (4 * (x % 2) + 2 * (y % 2) + lane_odd).astype(F32)
            hit = jnp.where(pooled(1, x // 2, y // 2) == code, mask, 0.0)
            chosen = jnp.where(total[y] + bias_two > 0, hit, 0.0)
            delta = jnp.where(chosen > 0, pooled(0, x // 2, y // 2), 0.0)
            put(s3, x + HALO, y + HALO, delta)
            out.append(delta)
        return out

    for x in range(px):
        rows = [choose(2 * x), choose(2 * x + 1)]
        for y in range(py):
            cells = [row[2 * y + k] for row in rows for k in range(2)]
            wide_w[x + 1, y + 1] = sum(cells).astype(BF)

    send(2)

    for x in range(cx):
        delta = s3[x + HALO, chans : 2 * chans, HALO * depth : (HALO + cy) * depth]
        grad(1, delta, s2, x, 0)

    pack(1)
    sum_start(1, 0)

    arrive(1, (True, False))
    arrive(2, (True, False))

    def put_delta(x, y):
        code = (4 * (x % 2) + 2 * (y % 2) + lane_odd).astype(F32)
        hit = wide_k[x // 2, y // 2].astype(F32) == code
        value = jnp.where(hit, wide_w[x // 2, y // 2].astype(F32), 0.0)
        put(s3, x, y, jnp.where(flags(x, y) > 0, value, 0.0))

    for x in range(cx + 2 * HALO):
        inner = HALO <= x < cx + HALO
        for y in (0, 1, cy + 2, cy + 3) if inner else range(cy + 2 * HALO):
            put_delta(x, y)

    def back(x):
        total = conv(w2b_ref, s3, x, 0, cy + 4, cy + 2, {})
        for y in range(cy + 2):
            hidden = s2[x, chans : 2 * chans, lanes_of(y)].astype(F32)
            put(s4, x, y, jnp.where(hidden > 0, total[y], 0.0))

    for x in range(cx + 2):
        back(x)
        if x == 4:
            sum_finish(1, 0)
            sum_start(1, 1)

    for x in range(cx):
        delta = s4[x + 1, chans : 2 * chans, depth : (1 + cy) * depth]
        grad(0, delta, s1, x + 1, 1)
        if x == 2:
            sum_finish(1, 1)
            sum_start(1, 2)

    pack(0)
    sum_start(0, 0)

    def last(x):
        total = conv(w1b_ref, s4, x, 0, cy + 2, cy, {})
        for y in range(cy):
            mask = flags(x + HALO, y + HALO)
            go[cell_rows(x, y), :] = jnp.where(mask > 0, total[y], 0.0)

    for x in range(cx):
        if x == 3:
            sum_finish(0, 0)
            sum_start(0, 1)
            sum_finish(1, 2)
            sum_start(1, 3)
        last(x)
    gin_ref[...] = go[...].reshape(chans, cx, cy, depth).astype(BF)

    sum_finish(1, 3)
    publish(1)
    sum_finish(0, 1)
    sum_start(0, 2)
    sum_finish(0, 2)
    sum_start(0, 3)
    sum_finish(0, 3)
    publish(0)

    for n in range(3):
        sent(n)
    for slot in range(2):
        for phase in range(4):
            for copy in sum_copies(slot, phase):
                copy.wait_send()


def body(features, occupancy, weight_one, bias_one, weight_two, bias_two, grad_pooled, pool_choice):
    chans, cx, cy, depth = features.shape
    nx, ny = lax.axis_size("gx"), lax.axis_size("gy")
    nz = nx // 2
    bx, by, bz = occupancy.shape
    lanes = -(-(9 * chans + 1) // 128) * 128

    def taps_first(weight):
        return weight.transpose(1, 2, 3, 0, 4).reshape(27, chans, chans)

    def vm(shape, dtype):
        return pltpu.VMEM(shape, dtype)

    px, py, half = grad_pooled.shape[1:]
    hbm = pl.BlockSpec(memory_space=pltpu.HBM)
    vmem = pl.BlockSpec(memory_space=pltpu.VMEM)
    gin, sums = pl.pallas_call(
        functools.partial(main_kernel, nx, ny, cx, cy, depth, chans),
        out_shape=(
            jax.ShapeDtypeStruct(features.shape, BF),
            jax.ShapeDtypeStruct((2, 28, chans, chans), F32),
        ),
        in_specs=[hbm] * 8,
        out_specs=(vmem,) * 2,
        scratch_shapes=[
            vm(features.shape, BF),
            vm(occupancy.shape, jnp.int32),
            vm((27, chans, chans), BF),
            vm((27, chans, chans), BF),
            vm((1, chans), F32),
            vm((1, chans), F32),
            vm(grad_pooled.shape, BF),
            vm(pool_choice.shape, jnp.int32),
            vm((chans * cx * cy, depth), F32),
            vm((chans * cx * cy, depth), F32),
            vm((2, chans * px * py, depth), F32),
            vm((lanes, 128), F32),
            vm((bx + 2, by + 2, depth), F32),
            vm((3 * chans, 9 * chans), BF),
            vm((3 * chans, 9 * chans), BF),
            vm((3 * chans, 9 * chans), BF),
            vm((3 * chans, 9 * chans), BF),
            vm((cx + 4, cy + 4, chans, depth), BF),
            vm((px + 2, py + 2, chans, depth), BF),
            vm((px + 2, py + 2, chans, depth), BF),
            vm((cx + 2, 4, chans, depth), F32),
            vm((cx, cy, chans, depth), F32),
            vm((cx + 4, 3 * chans, (cy + 4) * depth), BF),
            vm((cx + 2, 3 * chans, (cy + 2) * depth), BF),
            vm((cx + 4, 3 * chans, (cy + 4) * depth), BF),
            vm((cx + 2, 3 * chans, (cy + 2) * depth), BF),
            vm((2, chans, cy * depth), F32),
            vm((2, 3 * chans, lanes), F32),
            vm((2, 2, 3 * chans // 2, lanes), BF),
            vm((2, 3 * chans // 2, lanes), BF),
            vm((2, ny, 3 * chans // 2, lanes), BF),
            vm((2, nz, 3 * chans // 2, lanes), BF),
            vm((2, 2, 3 * chans // 2, lanes), BF),
            pltpu.SemaphoreType.DMA((8,)),
            pltpu.SemaphoreType.DMA((3, 8)),
            pltpu.SemaphoreType.DMA((3, 8)),
            pltpu.SemaphoreType.DMA((2, 4, max(ny, nz))),
            pltpu.SemaphoreType.DMA((2, 4, max(ny, nz))),
        ],
        compiler_params=pltpu.CompilerParams(
            collective_id=0, has_side_effects=True, vmem_limit_bytes=60 * 2**20
        ),
        name="main",
    )(
        features, occupancy, taps_first(weight_one), taps_first(weight_two),
        bias_one.reshape(1, chans), bias_two.reshape(1, chans), grad_pooled, pool_choice,
    )

    def taps_back(slot):
        return sums[slot, :27].reshape(3, 3, 3, chans, chans).transpose(3, 0, 1, 2, 4)

    return gin, taps_back(0), sums[0, 27, 0], taps_back(1), sums[1, 27, 0]


def solution(mesh):
    spread = P(None, "gx", "gy", None)
    return jax.shard_map(
        body,
        mesh=mesh,
        in_specs=(spread, P(), P(), P(), P(), P(), spread, spread),
        out_specs=(spread, P(), P(), P(), P()),
        check_vma=False,
    )
```

```python
import functools
import math

import jax
import jax.numpy as jnp
from jax import lax
from jax.experimental import pallas as pl
from jax.experimental.pallas import tpu as pltpu
from jax.sharding import PartitionSpec as P

MESH = pl.DeviceIdType.MESH
HALO = 2
SIDES = ((0, -1), (0, 1), (-1, -1), (-1, 1), (1, -1), (1, 1), (-1, 0), (1, 0))
BF = jnp.bfloat16
F32 = jnp.float32


def edge(side, cells, halo):
    if side == 0:
        return 0, cells
    return (0, halo) if side < 0 else (cells - halo, halo)


def landing(side, cells, halo):
    if side == 0:
        return halo
    return halo + cells if side < 0 else 0


def main_kernel(
    nx, ny, cx, cy, depth, chans,
    f_hbm, occ_hbm, w1_hbm, w2_hbm, b1_hbm, b2_hbm, gp_hbm, pc_hbm,
    gin_ref, sum_ref,
    f_ref, occ_ref, wn1_ref, wn2_ref, b1_ref, b2_ref, gp_ref, pc_ref,
    ft, go, pt, wt, mz_ref, w1_ref, w2_ref, w1b_ref, w2b_ref,
    wide_f, wide_k, wide_w, part1, part2, s1, s2, s3, s4, bias_acc, gw_ref,
    gs, r0, q1, q2, tot,
    local_sem, f_send, f_recv, send_sem, recv_sem, sum_send, sum_recv,
):
    gx = lax.axis_index("gx")
    gy = lax.axis_index("gy")
    nz = nx // 2
    core = lax.rem(gx, 2)
    gz = gx // 2
    taps = 27

    def exists(sx, sy):
        ok_x = jnp.logical_and(gx + sx >= 0, gx + sx < nx)
        ok_y = jnp.logical_and(gy + sy >= 0, gy + sy < ny)
        return jnp.logical_and(ok_x, ok_y)

    partner = (gx + 1 - 2 * core, gy)

    def peer_y(k):
        return (gx, lax.rem(gy + k, ny))

    def peer_z(k):
        return (2 * lax.rem(gz + k, nz) + core, gy)

    barrier = pltpu.get_barrier_semaphore()

    def greet(device):
        pl.semaphore_signal(barrier, inc=1, device_id=device, device_id_type=MESH)

    for k in range(1, nz):
        greet(peer_z(k))
    for k in range(1, ny):
        greet(peer_y(k))
    for sx, sy in SIDES:
        if sx:
            @pl.when(exists(sx, sy))
            def _():
                greet((gx + sx, gy + sy))
    beside_x = (gx > 0).astype(jnp.int32) + (gx < nx - 1).astype(jnp.int32)
    beside_y = (gy > 0).astype(jnp.int32) + (gy < ny - 1).astype(jnp.int32)

    local = [
        pltpu.make_async_copy(src, dst, local_sem.at[n])
        for n, (src, dst) in enumerate((
            (f_hbm, f_ref), (occ_hbm, occ_ref), (w1_hbm, wn1_ref), (w2_hbm, wn2_ref),
            (b1_hbm, b1_ref), (b2_hbm, b2_ref), (gp_hbm, gp_ref), (pc_hbm, pc_ref),
        ))
    ]
    for copy in local:
        copy.start()

    gw_ref[...] = jnp.zeros_like(gw_ref)
    bias_acc[...] = jnp.zeros_like(bias_acc)

    mz_ref[...] = jnp.zeros_like(mz_ref)
    local[1].wait()
    bz = occ_ref.shape[2]
    repeat = (
        lax.broadcasted_iota(jnp.int32, (bz, depth), 1) // (depth // bz)
        == lax.broadcasted_iota(jnp.int32, (bz, depth), 0)
    ).astype(BF)
    for bx in range(occ_ref.shape[0]):
        row = occ_ref[bx].astype(F32).astype(BF)
        mz_ref[bx + 1, 1 : 1 + occ_ref.shape[1], :] = jnp.dot(
            row, repeat, preferred_element_type=F32
        )

    def cell_rows(x, y):
        return pl.ds(x * cy + y, chans, stride=cx * cy)

    local[0].wait()
    ft[...] = f_ref[...].astype(F32).reshape(chans * cx * cy, depth)
    for x in range(cx):
        for y in range(cy):
            wide_f[x + HALO, y + HALO] = ft[cell_rows(x, y), :].astype(BF)

    pl.semaphore_wait(barrier, nz - 1 + ny - 1 + beside_x + beside_x * beside_y)

    def copy_of(n, k):
        sx, sy = SIDES[k]
        ref, halo, wx, wy = (wide_k, wide_w)[n], 1, cx // 2, cy // 2
        fx, lx = edge(sx, wx, halo)
        fy, ly = edge(sy, wy, halo)
        tx, ty = landing(sx, wx, halo), landing(sy, wy, halo)
        return pltpu.make_async_remote_copy(
            src_ref=ref.at[halo + fx : halo + fx + lx, halo + fy : halo + fy + ly],
            dst_ref=ref.at[tx : tx + lx, ty : ty + ly],
            send_sem=send_sem.at[n, k],
            recv_sem=recv_sem.at[n, k],
            device_id=(gx + sx, gy + sy),
            device_id_type=MESH,
        )

    def send(n):
        for k, (sx, sy) in enumerate(SIDES):
            @pl.when(exists(sx, sy))
            def _():
                copy_of(n, k).start()

    def arrive(n):
        for k, (sx, sy) in enumerate(SIDES):
            @pl.when(exists(-sx, -sy))
            def _():
                copy_of(n, k).wait_recv()

    def sent(n):
        for k, (sx, sy) in enumerate(SIDES):
            @pl.when(exists(sx, sy))
            def _():
                copy_of(n, k).wait_send()

    rows_apart = [HALO, cx] + list(range(2 * HALO, cx, HALO))

    def chunk(n, sy):
        fy = HALO if sy < 0 else cy
        ty = cy + HALO if sy < 0 else 0
        at = 2 * n + (sy > 0)
        x = rows_apart[n]
        return pltpu.make_async_remote_copy(
            src_ref=wide_f.at[x : x + HALO, fy : fy + HALO],
            dst_ref=wide_f.at[x : x + HALO, ty : ty + HALO],
            send_sem=f_send.at[at], recv_sem=f_recv.at[at],
            device_id=(gx, gy + sy), device_id_type=MESH,
        )

    def along_x(sx, sy):
        fx = HALO if sx < 0 else cx
        tx = cx + HALO if sx < 0 else 0
        y, count = (HALO, cy) if sy == 0 else (cy + HALO if sy < 0 else 0, HALO)
        at = 2 * len(rows_apart) + 2 * (sy % 3) + (sx > 0)
        return pltpu.make_async_remote_copy(
            src_ref=wide_f.at[fx : fx + HALO, y : y + count],
            dst_ref=wide_f.at[tx : tx + HALO, y : y + count],
            send_sem=f_send.at[at], recv_sem=f_recv.at[at],
            device_id=(gx + sx, gy), device_id_type=MESH,
        )

    for n in range(len(rows_apart)):
        for sy in (-1, 1):
            @pl.when(exists(0, sy))
            def _():
                chunk(n, sy).start()
        if n == 1:
            for sx in (-1, 1):
                @pl.when(exists(sx, 0))
                def _():
                    along_x(sx, 0).start()

    def take_chunk(n):
        for sy in (-1, 1):
            @pl.when(exists(0, -sy))
            def _():
                chunk(n, sy).wait_recv()
            for sx in (-1, 1):
                if n == (sx > 0):
                    @pl.when(exists(sx, -sy))
                    def _():
                        along_x(sx, sy).start()

    def take_x(sides):
        for sy in sides:
            for sx in (-1, 1):
                @pl.when(exists(-sx, -sy))
                def _():
                    along_x(sx, sy).wait_recv()

    def sent_f():
        for sy in (-1, 1):
            for n in range(len(rows_apart)):
                @pl.when(exists(0, sy))
                def _():
                    chunk(n, sy).wait_send()
        for sy in (0, -1, 1):
            for sx in (-1, 1):
                @pl.when(exists(sx, -sy))
                def _():
                    along_x(sx, sy).wait_send()

    for n, (nat, fwd, bwd) in enumerate(((wn1_ref, w1_ref, w1b_ref), (wn2_ref, w2_ref, w2b_ref))):
        local[2 + n].wait()
        wide = nat[...].astype(F32)
        for b in range(3):
            fwd[b * chans : (b + 1) * chans, :] = jnp.concatenate(
                [wide[a * 9 + b * 3 + c] for a in range(3) for c in range(3)], axis=1
            ).astype(BF)
        rows = wt.shape[0]
        wt[...] = jnp.zeros_like(wt)
        for a in range(3):
            for c in range(3):
                first = (a * 3 + c) * chans
                wt[first : first + chans, 0 : 3 * chans] = jnp.concatenate(
                    [wide[(2 - a) * 9 + (2 - b) * 3 + 2 - c] for b in range(3)], axis=1
                )
        turned = wt[...].T
        bwd[...] = turned[0 : 3 * chans, 0 : 9 * chans].astype(BF)

    half = depth // 2
    px, py = cx // 2, cy // 2
    spread = (
        lax.broadcasted_iota(jnp.int32, (half, depth), 1) // 2
        == lax.broadcasted_iota(jnp.int32, (half, depth), 0)
    ).astype(BF)
    local[6].wait()
    local[7].wait()
    for n, ref in enumerate((gp_ref, pc_ref)):
        for c in range(chans):
            for x in range(px):
                first = (c * px + x) * py
                pt[n, first : first + py, 0:half] = ref[c, x].astype(F32)
        pt[n] = jnp.dot(pt[n, :, 0:half].astype(BF), spread, preferred_element_type=F32)

    def pooled(n, x, y):
        return pt[n, pl.ds(x * py + y, chans, stride=px * py), :]

    for x in range(px):
        for y in range(py):
            wide_k[x + 1, y + 1] = pooled(1, x, y).astype(BF)

    same = lax.broadcasted_iota(jnp.int32, (chans, chans), 0) == lax.broadcasted_iota(
        jnp.int32, (chans, chans), 1
    )
    local[4].wait()
    local[5].wait()
    bias_one, bias_two = [
        jnp.sum(jnp.where(same, ref[...], 0.0), axis=1, keepdims=True) for ref in (b1_ref, b2_ref)
    ]
    lane = lax.broadcasted_iota(jnp.int32, (1, depth), 1)
    not_first = lane != 0
    not_last = lane != depth - 1
    lane_odd = lane % 2

    def flags(x, y):
        brick = gx * (cx // 8) + (x + 8 - HALO) // 8
        return mz_ref[brick, pl.ds(gy * (cy // 8) + (y + 8 - HALO) // 8, 1), :]

    def lanes_of(y, count=1):
        return slice(y * depth, (y + count) * depth)

    def put(stack, x, y, value):
        rounded = value.astype(BF)
        wide = rounded.astype(F32)
        where = lanes_of(y)
        stack[x, 0:chans, where] = jnp.where(not_first, pltpu.roll(wide, 1, 1), 0.0).astype(BF)
        stack[x, chans : 2 * chans, where] = rounded
        stack[x, 2 * chans : 3 * chans, where] = jnp.where(
            not_last, pltpu.roll(wide, depth - 1, 1), 0.0
        ).astype(BF)
        return rounded

    def put_cell(x, y):
        put(s1, x, y, jnp.where(flags(x, y) > 0, wide_f[x, y].astype(F32), 0.0))

    def conv(weight, stack, x, first, count, outs, total):
        rows = stack[pl.ds(x, 3), :, lanes_of(first, count)].reshape(9 * chans, count * depth)
        full = jnp.dot(weight[...], rows, preferred_element_type=F32)
        for t in range(count):
            for b in range(3):
                y = first + t - b
                if 0 <= y < outs:
                    piece = full[b * chans : (b + 1) * chans, lanes_of(t)]
                    total[y] = total[y] + piece if y in total else piece
        return total

    def grad(slot, delta, stack, x, first):
        width = (cy + 2) * depth
        rows = stack[pl.ds(x, 3), :, first * depth : first * depth + width].reshape(9 * chans, width)
        shifted = []
        for b in range(3):
            parts = []
            if b:
                parts.append(jnp.zeros((chans, b * depth), BF))
            parts.append(delta)
            if b < 2:
                parts.append(jnp.zeros((chans, (2 - b) * depth), BF))
            shifted.append(jnp.concatenate(parts, axis=1))
        left = jnp.concatenate(shifted, axis=0)
        gw_ref[slot, :, 0 : 9 * chans] += lax.dot_general(
            left, rows, (((1,), (1,)), ((), ())), preferred_element_type=F32
        )
        bias_acc[slot] += delta.astype(F32)

    part_rows = 3 * chans // 2

    def pack(slot):
        total = jnp.sum(bias_acc[slot], axis=1, keepdims=True)
        gw_ref[slot, 0:chans, 9 * chans :] = jnp.broadcast_to(
            total, (chans, gw_ref.shape[2] - 9 * chans)
        )
        for n in range(2):
            gs[slot, n] = gw_ref[slot, n * part_rows : (n + 1) * part_rows].astype(BF)

    def sum_copies(slot, phase):
        if phase == 0:
            moves = [(gs.at[slot, 1 - core], r0.at[slot], partner)]
        elif phase == 1:
            moves = [(q1.at[slot, gy], q1.at[slot, gy], peer_y(k)) for k in range(1, ny)]
        elif phase == 2:
            moves = [(q2.at[slot, gz], q2.at[slot, gz], peer_z(k)) for k in range(1, nz)]
        else:
            moves = [(tot.at[slot, core], tot.at[slot, core], partner)]
        return [
            pltpu.make_async_remote_copy(
                src_ref=src, dst_ref=dst,
                send_sem=sum_send.at[slot, phase, k], recv_sem=sum_recv.at[slot, phase, k],
                device_id=device, device_id_type=MESH,
            )
            for k, (src, dst, device) in enumerate(moves)
        ]

    def sum_start(slot, phase):
        for copy in sum_copies(slot, phase):
            copy.start()

    def sum_finish(slot, phase):
        for copy in sum_copies(slot, phase):
            copy.wait_recv()
        if phase == 0:
            q1[slot, gy] = (gs[slot, core].astype(F32) + r0[slot].astype(F32)).astype(BF)
        if phase == 1:
            q2[slot, gz] = sum(q1[slot, k].astype(F32) for k in range(ny)).astype(BF)
        if phase == 2:
            tot[slot, core] = sum(q2[slot, k].astype(F32) for k in range(nz)).astype(BF)

    scale = 1.0 / math.sqrt(cx * nx * cy * ny * depth)

    def publish(slot):
        full = jnp.concatenate([tot[slot, 0], tot[slot, 1]], axis=0).astype(F32) * scale
        for b in range(3):
            for a in range(3):
                for c in range(3):
                    first = (a * 3 + c) * chans
                    sum_ref[slot, a * 9 + b * 3 + c] = full[b * chans : (b + 1) * chans, first : first + chans]
        column = full[0:chans, 9 * chans : 10 * chans]
        row = jnp.sum(jnp.where(same, column, 0.0), axis=0, keepdims=True)
        sum_ref[slot, taps] = jnp.broadcast_to(row, (chans, chans))

    for x in range(cx):
        for y in range(cy):
            put_cell(x + HALO, y + HALO)

    def early_one(x):
        total = conv(w1_ref, s1, x, HALO, cy, cy + 2, {})
        for y in range(2, cy):
            hide(x, y, total[y])
        for n, y in enumerate((0, 1, cy, cy + 1)):
            part1[x, n] = total[y]

    def hide(x, y, pre):
        mask = flags(x + 1, y + 1)
        put(s2, x, y, jnp.where(mask > 0, jnp.maximum(pre + bias_one, 0.0), 0.0))

    for x in range(2, cx):
        early_one(x)
    take_x((0,))
    for n in (0, 1, cx + 2, cx + 3):
        for y in range(cy):
            put_cell(n, y + HALO)
    for x in (0, 1, cx, cx + 1):
        early_one(x)

    def early_two(x):
        total = conv(w2_ref, s2, x, 2, cy - 2, cy, {})
        for y in range(cy):
            part2[x, y] = total[y]

    for x in range(cx):
        early_two(x)

    edges = (0, 1, cy, cy + 1)

    def late_one(x):
        total = {y: part1[x, n] for n, y in enumerate(edges)}
        conv(w1_ref, s1, x, 0, 2, cy + 2, total)
        conv(w1_ref, s1, x, cy + 2, 2, cy + 2, total)
        for y in edges:
            hide(x, y, total[y])

    def put_rows(x):
        for n in range(x, x + HALO):
            for y in (0, 1, cy + 2, cy + 3):
                put_cell(n, y)

    for n, x in enumerate(rows_apart):
        take_chunk(n)
        if n:
            for first in rows_apart[n - 1 : n + 1] if n == 1 else (x,):
                put_rows(first)
    send(0)
    for x in range(2, cx):
        late_one(x)
    take_x((-1, 1))
    for x in (0, cx + HALO):
        put_rows(x)
    for x in (0, 1, cx, cx + 1):
        late_one(x)

    def choose(x):
        total = {y: part2[x, y] for y in range(cy)}
        conv(w2_ref, s2, x, 0, 2, cy, total)
        conv(w2_ref, s2, x, cy, 2, cy, total)
        out = []
        for y in range(cy):
            mask = flags(x + HALO, y + HALO)
            code = (4 * (x % 2) + 2 * (y % 2) + lane_odd).astype(F32)
            hit = jnp.where(pooled(1, x // 2, y // 2) == code, mask, 0.0)
            chosen = jnp.where(total[y] + bias_two > 0, hit, 0.0)
            delta = jnp.where(chosen > 0, pooled(0, x // 2, y // 2), 0.0)
            put(s3, x + HALO, y + HALO, delta)
            out.append(delta)
        return out

    for x in [*range(1, px - 1), 0, px - 1]:
        rows = [choose(2 * x), choose(2 * x + 1)]
        for y in range(py):
            cells = [row[2 * y + k] for row in rows for k in range(2)]
            wide_w[x + 1, y + 1] = sum(cells).astype(BF)

    send(1)

    for x in range(cx):
        delta = s3[x + HALO, chans : 2 * chans, HALO * depth : (HALO + cy) * depth]
        grad(1, delta, s2, x, 0)

    pack(1)
    sum_start(1, 0)

    def put_delta(x, y):
        code = (4 * (x % 2) + 2 * (y % 2) + lane_odd).astype(F32)
        hit = wide_k[x // 2, y // 2].astype(F32) == code
        value = jnp.where(hit, wide_w[x // 2, y // 2].astype(F32), 0.0)
        put(s3, x, y, jnp.where(flags(x, y) > 0, value, 0.0))

    def put_back(x, y, total):
        hidden = s2[x, chans : 2 * chans, lanes_of(y)].astype(F32)
        put(s4, x, y, jnp.where(hidden > 0, total, 0.0))

    def early_back(x):
        total = conv(w2b_ref, s3, x, HALO, cy, cy + 2, {})
        for y in range(2, cy):
            put_back(x, y, total[y])
        for n, y in enumerate(edges):
            part1[x, n] = total[y]

    def late_back(x):
        total = {y: part1[x, n] for n, y in enumerate(edges)}
        conv(w2b_ref, s3, x, 0, 2, cy + 2, total)
        conv(w2b_ref, s3, x, cy + 2, 2, cy + 2, total)
        for y in edges:
            put_back(x, y, total[y])

    def back(x):
        total = conv(w2b_ref, s3, x, 0, cy + 4, cy + 2, {})
        for y in range(cy + 2):
            put_back(x, y, total[y])

    for x in range(2, cx):
        early_back(x)

    arrive(0)
    arrive(1)
    sum_finish(1, 0)
    sum_start(1, 1)
    for x in range(cx + 2 * HALO):
        inner = HALO <= x < cx + HALO
        for y in (0, 1, cy + 2, cy + 3) if inner else range(cy + 2 * HALO):
            put_delta(x, y)
    for x in range(2, cx):
        late_back(x)
    for x in (0, 1, cx, cx + 1):
        back(x)

    for x in range(cx):
        delta = s4[x + 1, chans : 2 * chans, depth : (1 + cy) * depth]
        grad(0, delta, s1, x + 1, 1)

    pack(0)
    sum_start(0, 0)
    sum_finish(1, 1)
    sum_start(1, 2)

    def last(x):
        total = conv(w1b_ref, s4, x, 0, cy + 2, cy, {})
        for y in range(cy):
            mask = flags(x + HALO, y + HALO)
            go[cell_rows(x, y), :] = jnp.where(mask > 0, total[y], 0.0)

    for x in range(cx):
        if x == cx // 2:
            sum_finish(0, 0)
            sum_start(0, 1)
        last(x)
    gin_ref[...] = go[...].reshape(chans, cx, cy, depth).astype(BF)

    sum_finish(1, 2)
    sum_start(1, 3)
    sum_finish(0, 1)
    sum_start(0, 2)
    sum_finish(1, 3)
    publish(1)
    sum_finish(0, 2)
    sum_start(0, 3)
    sum_finish(0, 3)
    publish(0)

    sent_f()
    for n in range(2):
        sent(n)
    for slot in range(2):
        for phase in range(4):
            for copy in sum_copies(slot, phase):
                copy.wait_send()


def body(features, occupancy, weight_one, bias_one, weight_two, bias_two, grad_pooled, pool_choice):
    chans, cx, cy, depth = features.shape
    nx, ny = lax.axis_size("gx"), lax.axis_size("gy")
    nz = nx // 2
    bx, by, bz = occupancy.shape
    lanes = -(-(9 * chans + 1) // 128) * 128

    def taps_first(weight):
        return weight.transpose(1, 2, 3, 0, 4).reshape(27, chans, chans)

    def vm(shape, dtype):
        return pltpu.VMEM(shape, dtype)

    px, py, half = grad_pooled.shape[1:]
    hbm = pl.BlockSpec(memory_space=pltpu.HBM)
    vmem = pl.BlockSpec(memory_space=pltpu.VMEM)
    gin, sums = pl.pallas_call(
        functools.partial(main_kernel, nx, ny, cx, cy, depth, chans),
        out_shape=(
            jax.ShapeDtypeStruct(features.shape, BF),
            jax.ShapeDtypeStruct((2, 28, chans, chans), F32),
        ),
        in_specs=[hbm] * 8,
        out_specs=(vmem,) * 2,
        scratch_shapes=[
            vm(features.shape, BF),
            vm(occupancy.shape, jnp.int32),
            vm((27, chans, chans), BF),
            vm((27, chans, chans), BF),
            vm((1, chans), F32),
            vm((1, chans), F32),
            vm(grad_pooled.shape, BF),
            vm(pool_choice.shape, jnp.int32),
            vm((chans * cx * cy, depth), F32),
            vm((chans * cx * cy, depth), F32),
            vm((2, chans * px * py, depth), F32),
            vm((lanes, 128), F32),
            vm((bx + 2, by + 2, depth), F32),
            vm((3 * chans, 9 * chans), BF),
            vm((3 * chans, 9 * chans), BF),
            vm((3 * chans, 9 * chans), BF),
            vm((3 * chans, 9 * chans), BF),
            vm((cx + 4, cy + 4, chans, depth), BF),
            vm((px + 2, py + 2, chans, depth), BF),
            vm((px + 2, py + 2, chans, depth), BF),
            vm((cx + 2, 4, chans, depth), F32),
            vm((cx, cy, chans, depth), F32),
            vm((cx + 4, 3 * chans, (cy + 4) * depth), BF),
            vm((cx + 2, 3 * chans, (cy + 2) * depth), BF),
            vm((cx + 4, 3 * chans, (cy + 4) * depth), BF),
            vm((cx + 2, 3 * chans, (cy + 2) * depth), BF),
            vm((2, chans, cy * depth), F32),
            vm((2, 3 * chans, lanes), F32),
            vm((2, 2, 3 * chans // 2, lanes), BF),
            vm((2, 3 * chans // 2, lanes), BF),
            vm((2, ny, 3 * chans // 2, lanes), BF),
            vm((2, nz, 3 * chans // 2, lanes), BF),
            vm((2, 2, 3 * chans // 2, lanes), BF),
            pltpu.SemaphoreType.DMA((8,)),
            pltpu.SemaphoreType.DMA((2 * (cx // HALO) + 6,)),
            pltpu.SemaphoreType.DMA((2 * (cx // HALO) + 6,)),
            pltpu.SemaphoreType.DMA((2, 8)),
            pltpu.SemaphoreType.DMA((2, 8)),
            pltpu.SemaphoreType.DMA((2, 4, max(ny, nz))),
            pltpu.SemaphoreType.DMA((2, 4, max(ny, nz))),
        ],
        compiler_params=pltpu.CompilerParams(
            collective_id=0, has_side_effects=True, vmem_limit_bytes=48 * 2**20
        ),
        name="main",
    )(*[pltpu.with_memory_space_constraint(v, pltpu.HBM) for v in (
        features, occupancy, taps_first(weight_one), taps_first(weight_two),
        bias_one.reshape(1, chans), bias_two.reshape(1, chans), grad_pooled, pool_choice,
    )])

    def taps_back(slot):
        return sums[slot, :27].reshape(3, 3, 3, chans, chans).transpose(3, 0, 1, 2, 4)

    return gin, taps_back(0), sums[0, 27, 0], taps_back(1), sums[1, 27, 0]


def solution(mesh):
    spread = P(None, "gx", "gy", None)
    return jax.shard_map(
        body,
        mesh=mesh,
        in_specs=(spread, P(), P(), P(), P(), P(), spread, spread),
        out_specs=(spread, P(), P(), P(), P()),
        check_vma=False,
    )
```

```python
import functools
import math

import jax
import jax.numpy as jnp
from jax import lax
from jax.experimental import pallas as pl
from jax.experimental.pallas import tpu as pltpu
from jax.sharding import PartitionSpec as P

MESH = pl.DeviceIdType.MESH
HALO = 2
SPARE = 16
SIDES = ((0, -1), (0, 1), (-1, -1), (-1, 1), (1, -1), (1, 1), (-1, 0), (1, 0))
BF = jnp.bfloat16
F32 = jnp.float32


def edge(side, cells, halo):
    if side == 0:
        return 0, cells
    return (0, halo) if side < 0 else (cells - halo, halo)


def landing(side, cells, halo):
    if side == 0:
        return halo
    return halo + cells if side < 0 else 0


def main_kernel(
    nx, ny, cx, cy, depth, chans,
    f_hbm, occ_hbm, w1_hbm, w2_hbm, b1_hbm, b2_hbm, gp_hbm, pc_hbm,
    gin_ref, tot,
    f_ref, occ_ref, wn1_ref, wn2_ref, b1_ref, b2_ref, gp_ref, pc_ref,
    ft, go, pt, wt, mz_ref, w1_ref, w2_ref, w1b_ref, w2b_ref,
    wide_f, wide_k, wide_w, part1, part2, s1, s2, s3, s4, gw_ref,
    gs, r0, q1, q2,
    local_sem, f_send, f_recv, send_sem, recv_sem, sum_send, sum_recv,
):
    gx = lax.axis_index("gx")
    gy = lax.axis_index("gy")
    nz = nx // 2
    core = lax.rem(gx, 2)
    gz = gx // 2

    def exists(sx, sy):
        ok_x = jnp.logical_and(gx + sx >= 0, gx + sx < nx)
        ok_y = jnp.logical_and(gy + sy >= 0, gy + sy < ny)
        return jnp.logical_and(ok_x, ok_y)

    partner = (gx + 1 - 2 * core, gy)

    def peer_y(k):
        return (gx, lax.rem(gy + k, ny))

    def peer_z(k):
        return (2 * lax.rem(gz + k, nz) + core, gy)

    barrier = pltpu.get_barrier_semaphore()

    def greet(device):
        pl.semaphore_signal(barrier, inc=1, device_id=device, device_id_type=MESH)

    for k in range(1, nz):
        greet(peer_z(k))
    for k in range(1, ny):
        greet(peer_y(k))
    for sx, sy in SIDES:
        if sx:
            @pl.when(exists(sx, sy))
            def _():
                greet((gx + sx, gy + sy))
    beside_x = (gx > 0).astype(jnp.int32) + (gx < nx - 1).astype(jnp.int32)
    beside_y = (gy > 0).astype(jnp.int32) + (gy < ny - 1).astype(jnp.int32)

    local = [
        pltpu.make_async_copy(src, dst, local_sem.at[n])
        for n, (src, dst) in enumerate((
            (f_hbm, f_ref), (occ_hbm, occ_ref), (w1_hbm, wn1_ref), (w2_hbm, wn2_ref),
            (b1_hbm, b1_ref), (b2_hbm, b2_ref), (gp_hbm, gp_ref), (pc_hbm, pc_ref),
        ))
    ]
    for copy in local:
        copy.start()

    gw_ref[...] = jnp.zeros_like(gw_ref)

    mz_ref[...] = jnp.zeros_like(mz_ref)
    local[1].wait()
    bz = occ_ref.shape[2]
    repeat = (
        lax.broadcasted_iota(jnp.int32, (bz, depth), 1) // (depth // bz)
        == lax.broadcasted_iota(jnp.int32, (bz, depth), 0)
    ).astype(BF)
    for bx in range(occ_ref.shape[0]):
        row = occ_ref[bx].astype(F32).astype(BF)
        mz_ref[bx + 1, 1 : 1 + occ_ref.shape[1], :] = jnp.dot(
            row, repeat, preferred_element_type=F32
        )

    def cell_rows(x, y):
        return pl.ds(x * cy + y, chans, stride=cx * cy)

    local[0].wait()
    ft[...] = f_ref[...].astype(F32).reshape(chans * cx * cy, depth)
    for x in range(cx):
        for y in range(cy):
            wide_f[x + HALO, y + HALO] = ft[cell_rows(x, y), :].astype(BF)

    pl.semaphore_wait(barrier, nz - 1 + ny - 1 + beside_x + beside_x * beside_y)

    def copy_of(n, k):
        sx, sy = SIDES[k]
        ref, halo, wx, wy = (wide_k, wide_w)[n], 1, cx // 2, cy // 2
        fx, lx = edge(sx, wx, halo)
        fy, ly = edge(sy, wy, halo)
        tx, ty = landing(sx, wx, halo), landing(sy, wy, halo)
        return pltpu.make_async_remote_copy(
            src_ref=ref.at[halo + fx : halo + fx + lx, halo + fy : halo + fy + ly],
            dst_ref=ref.at[tx : tx + lx, ty : ty + ly],
            send_sem=send_sem.at[n, k],
            recv_sem=recv_sem.at[n, k],
            device_id=(gx + sx, gy + sy),
            device_id_type=MESH,
        )

    def send(n):
        for k, (sx, sy) in enumerate(SIDES):
            @pl.when(exists(sx, sy))
            def _():
                copy_of(n, k).start()

    def arrive(n):
        for k, (sx, sy) in enumerate(SIDES):
            @pl.when(exists(-sx, -sy))
            def _():
                copy_of(n, k).wait_recv()

    def sent(n):
        for k, (sx, sy) in enumerate(SIDES):
            @pl.when(exists(sx, sy))
            def _():
                copy_of(n, k).wait_send()

    rows_apart = [HALO, cx] + list(range(2 * HALO, cx, HALO))

    def chunk(n, sy):
        fy = HALO if sy < 0 else cy
        ty = cy + HALO if sy < 0 else 0
        at = 2 * n + (sy > 0)
        x = rows_apart[n]
        return pltpu.make_async_remote_copy(
            src_ref=wide_f.at[x : x + HALO, fy : fy + HALO],
            dst_ref=wide_f.at[x : x + HALO, ty : ty + HALO],
            send_sem=f_send.at[at], recv_sem=f_recv.at[at],
            device_id=(gx, gy + sy), device_id_type=MESH,
        )

    def along_x(sx, sy):
        fx = HALO if sx < 0 else cx
        tx = cx + HALO if sx < 0 else 0
        y, count = (HALO, cy) if sy == 0 else (cy + HALO if sy < 0 else 0, HALO)
        at = 2 * len(rows_apart) + 2 * (sy % 3) + (sx > 0)
        return pltpu.make_async_remote_copy(
            src_ref=wide_f.at[fx : fx + HALO, y : y + count],
            dst_ref=wide_f.at[tx : tx + HALO, y : y + count],
            send_sem=f_send.at[at], recv_sem=f_recv.at[at],
            device_id=(gx + sx, gy), device_id_type=MESH,
        )

    for n in range(len(rows_apart)):
        for sy in (-1, 1):
            @pl.when(exists(0, sy))
            def _():
                chunk(n, sy).start()
        if n == 1:
            for sx in (-1, 1):
                @pl.when(exists(sx, 0))
                def _():
                    along_x(sx, 0).start()

    def take_chunk(n):
        for sy in (-1, 1):
            @pl.when(exists(0, -sy))
            def _():
                chunk(n, sy).wait_recv()
            for sx in (-1, 1):
                if n == (sx > 0):
                    @pl.when(exists(sx, -sy))
                    def _():
                        along_x(sx, sy).start()

    def take_x(sides):
        for sy in sides:
            for sx in (-1, 1):
                @pl.when(exists(-sx, -sy))
                def _():
                    along_x(sx, sy).wait_recv()

    def sent_f():
        for sy in (-1, 1):
            for n in range(len(rows_apart)):
                @pl.when(exists(0, sy))
                def _():
                    chunk(n, sy).wait_send()
        for sy in (0, -1, 1):
            for sx in (-1, 1):
                @pl.when(exists(sx, -sy))
                def _():
                    along_x(sx, sy).wait_send()

    for n, (nat, fwd, bwd) in enumerate(((wn1_ref, w1_ref, w1b_ref), (wn2_ref, w2_ref, w2b_ref))):
        local[2 + n].wait()
        wide = nat[...].astype(F32)
        for b in range(3):
            fwd[b * chans : (b + 1) * chans, :] = jnp.concatenate(
                [wide[a * 9 + b * 3 + c] for a in range(3) for c in range(3)], axis=1
            ).astype(BF)
        rows = wt.shape[0]
        wt[...] = jnp.zeros_like(wt)
        for a in range(3):
            for c in range(3):
                first = (a * 3 + c) * chans
                wt[first : first + chans, 0 : 3 * chans] = jnp.concatenate(
                    [wide[(2 - a) * 9 + (2 - b) * 3 + 2 - c] for b in range(3)], axis=1
                )
        turned = wt[...].T
        bwd[...] = turned[0 : 3 * chans, 0 : 9 * chans].astype(BF)

    half = depth // 2
    px, py = cx // 2, cy // 2
    spread = (
        lax.broadcasted_iota(jnp.int32, (half, depth), 1) // 2
        == lax.broadcasted_iota(jnp.int32, (half, depth), 0)
    ).astype(BF)
    local[6].wait()
    local[7].wait()
    for n, ref in enumerate((gp_ref, pc_ref)):
        for c in range(chans):
            for x in range(px):
                first = (c * px + x) * py
                pt[n, first : first + py, 0:half] = ref[c, x].astype(F32)
        pt[n] = jnp.dot(pt[n, :, 0:half].astype(BF), spread, preferred_element_type=F32)

    def pooled(n, x, y):
        return pt[n, pl.ds(x * py + y, chans, stride=px * py), :]

    for x in range(px):
        for y in range(py):
            wide_k[x + 1, y + 1] = pooled(1, x, y).astype(BF)

    same = lax.broadcasted_iota(jnp.int32, (chans, chans), 0) == lax.broadcasted_iota(
        jnp.int32, (chans, chans), 1
    )
    local[4].wait()
    local[5].wait()
    bias_one, bias_two = [
        jnp.sum(jnp.where(same, ref[...], 0.0), axis=1, keepdims=True) for ref in (b1_ref, b2_ref)
    ]
    lane = lax.broadcasted_iota(jnp.int32, (1, depth), 1)
    not_first = lane != 0
    not_last = lane != depth - 1
    lane_odd = lane % 2

    def flags(x, y):
        brick = gx * (cx // 8) + (x + 8 - HALO) // 8
        return mz_ref[brick, pl.ds(gy * (cy // 8) + (y + 8 - HALO) // 8, 1), :]

    def lanes_of(y, count=1):
        return slice(y * depth, (y + count) * depth)

    def put(stack, x, y, value):
        rounded = value.astype(BF)
        wide = rounded.astype(F32)
        where = lanes_of(y)
        stack[x, 0:chans, where] = jnp.where(not_first, pltpu.roll(wide, 1, 1), 0.0).astype(BF)
        stack[x, chans : 2 * chans, where] = rounded
        stack[x, 2 * chans : 3 * chans, where] = jnp.where(
            not_last, pltpu.roll(wide, depth - 1, 1), 0.0
        ).astype(BF)
        return rounded

    def put_cell(x, y):
        put(s1, x, y, jnp.where(flags(x, y) > 0, wide_f[x, y].astype(F32), 0.0))

    def conv(weight, stack, x, first, count, outs, total):
        rows = stack[pl.ds(x, 3), :, lanes_of(first, count)].reshape(9 * chans, count * depth)
        full = jnp.dot(weight[...], rows, preferred_element_type=F32)
        for t in range(count):
            for b in range(3):
                y = first + t - b
                if 0 <= y < outs:
                    piece = full[b * chans : (b + 1) * chans, lanes_of(t)]
                    total[y] = total[y] + piece if y in total else piece
        return total

    def grad(slot, delta, stack, x, first):
        width = (cy + 2) * depth
        rows = stack[pl.ds(x, 3), :, first * depth : first * depth + width].reshape(9 * chans, width)
        shifted = []
        for b in range(3):
            parts = []
            if b:
                parts.append(jnp.zeros((chans, b * depth), BF))
            parts.append(delta)
            if b < 2:
                parts.append(jnp.zeros((chans, (2 - b) * depth), BF))
            shifted.append(jnp.concatenate(parts, axis=1))
        left = jnp.concatenate(shifted, axis=0)
        right = jnp.concatenate([rows, jnp.ones((SPARE, width), BF)], axis=0)
        gw_ref[slot, :, 0 : 3 * chans] += lax.dot_general(
            right, left, (((1,), (1,)), ((), ())), preferred_element_type=F32
        )

    def pack(slot):
        total = gw_ref[slot]

        def block(n, b):
            return total[n * chans : (n + 1) * chans, b * chans : (b + 1) * chans]

        last = [block(n, b) for n in (7, 8) for b in range(3)]
        last.append(jnp.broadcast_to(total[9 * chans : 9 * chans + 1, 0:chans], (chans, chans)))
        full = jnp.concatenate(
            [
                jnp.concatenate([total[n * chans : (n + 1) * chans, 0 : 3 * chans], last[n]], axis=1)
                for n in range(7)
            ],
            axis=0,
        )
        gs[slot] = full.reshape(gs.shape[1:]).astype(BF)

    def sum_copies(slot, phase):
        if phase == 0:
            moves = [(gs.at[slot, 1 - core], r0.at[slot], partner)]
        elif phase == 1:
            moves = [(q1.at[slot, gy], q1.at[slot, gy], peer_y(k)) for k in range(1, ny)]
        elif phase == 2:
            moves = [(q2.at[slot, gz], q2.at[slot, gz], peer_z(k)) for k in range(1, nz)]
        else:
            moves = [(tot.at[slot, core], tot.at[slot, core], partner)]
        return [
            pltpu.make_async_remote_copy(
                src_ref=src, dst_ref=dst,
                send_sem=sum_send.at[slot, phase, k], recv_sem=sum_recv.at[slot, phase, k],
                device_id=device, device_id_type=MESH,
            )
            for k, (src, dst, device) in enumerate(moves)
        ]

    def sum_start(slot, phase):
        for copy in sum_copies(slot, phase):
            copy.start()

    def sum_finish(slot, phase):
        for copy in sum_copies(slot, phase):
            copy.wait_recv()
        if phase == 0:
            q1[slot, gy] = (gs[slot, core].astype(F32) + r0[slot].astype(F32)).astype(BF)
        if phase == 1:
            q2[slot, gz] = sum(q1[slot, k].astype(F32) for k in range(ny)).astype(BF)
        if phase == 2:
            tot[slot, core] = sum(q2[slot, k].astype(F32) for k in range(nz)).astype(BF)

    for x in range(cx):
        for y in range(cy):
            put_cell(x + HALO, y + HALO)

    def early_one(x):
        total = conv(w1_ref, s1, x, HALO, cy, cy + 2, {})
        for y in range(2, cy):
            hide(x, y, total[y])
        for n, y in enumerate((0, 1, cy, cy + 1)):
            part1[x, n] = total[y]

    def hide(x, y, pre):
        mask = flags(x + 1, y + 1)
        put(s2, x, y, jnp.where(mask > 0, jnp.maximum(pre + bias_one, 0.0), 0.0))

    for x in range(2, cx):
        early_one(x)
    take_x((0,))
    for n in (0, 1, cx + 2, cx + 3):
        for y in range(cy):
            put_cell(n, y + HALO)
    for x in (0, 1, cx, cx + 1):
        early_one(x)

    def early_two(x):
        total = conv(w2_ref, s2, x, 2, cy - 2, cy, {})
        for y in range(cy):
            part2[x, y] = total[y]

    for x in range(cx):
        early_two(x)

    edges = (0, 1, cy, cy + 1)

    def late_one(x):
        total = {y: part1[x, n] for n, y in enumerate(edges)}
        conv(w1_ref, s1, x, 0, 2, cy + 2, total)
        conv(w1_ref, s1, x, cy + 2, 2, cy + 2, total)
        for y in edges:
            hide(x, y, total[y])

    def put_rows(x):
        for n in range(x, x + HALO):
            for y in (0, 1, cy + 2, cy + 3):
                put_cell(n, y)

    for n, x in enumerate(rows_apart):
        take_chunk(n)
        if n:
            for first in rows_apart[n - 1 : n + 1] if n == 1 else (x,):
                put_rows(first)
    send(0)
    for x in range(2, cx):
        late_one(x)
    take_x((-1, 1))
    for x in (0, cx + HALO):
        put_rows(x)
    for x in (0, 1, cx, cx + 1):
        late_one(x)

    def choose(x):
        total = {y: part2[x, y] for y in range(cy)}
        conv(w2_ref, s2, x, 0, 2, cy, total)
        conv(w2_ref, s2, x, cy, 2, cy, total)
        out = []
        for y in range(cy):
            mask = flags(x + HALO, y + HALO)
            code = (4 * (x % 2) + 2 * (y % 2) + lane_odd).astype(F32)
            hit = jnp.where(pooled(1, x // 2, y // 2) == code, mask, 0.0)
            chosen = jnp.where(total[y] + bias_two > 0, hit, 0.0)
            delta = jnp.where(chosen > 0, pooled(0, x // 2, y // 2), 0.0)
            put(s3, x + HALO, y + HALO, delta)
            out.append(delta)
        return out

    for x in [*range(1, px - 1), 0, px - 1]:
        rows = [choose(2 * x), choose(2 * x + 1)]
        for y in range(py):
            cells = [row[2 * y + k] for row in rows for k in range(2)]
            wide_w[x + 1, y + 1] = sum(cells).astype(BF)

    send(1)

    for x in range(cx):
        delta = s3[x + HALO, chans : 2 * chans, HALO * depth : (HALO + cy) * depth]
        grad(1, delta, s2, x, 0)

    pack(1)
    sum_start(1, 0)

    def put_delta(x, y):
        code = (4 * (x % 2) + 2 * (y % 2) + lane_odd).astype(F32)
        hit = wide_k[x // 2, y // 2].astype(F32) == code
        value = jnp.where(hit, wide_w[x // 2, y // 2].astype(F32), 0.0)
        put(s3, x, y, jnp.where(flags(x, y) > 0, value, 0.0))

    def put_back(x, y, total):
        hidden = s2[x, chans : 2 * chans, lanes_of(y)].astype(F32)
        put(s4, x, y, jnp.where(hidden > 0, total, 0.0))

    def early_back(x):
        total = conv(w2b_ref, s3, x, HALO, cy, cy + 2, {})
        for y in range(2, cy):
            put_back(x, y, total[y])
        for n, y in enumerate(edges):
            part1[x, n] = total[y]

    def late_back(x):
        total = {y: part1[x, n] for n, y in enumerate(edges)}
        conv(w2b_ref, s3, x, 0, 2, cy + 2, total)
        conv(w2b_ref, s3, x, cy + 2, 2, cy + 2, total)
        for y in edges:
            put_back(x, y, total[y])

    def back(x):
        total = conv(w2b_ref, s3, x, 0, cy + 4, cy + 2, {})
        for y in range(cy + 2):
            put_back(x, y, total[y])

    for x in range(2, cx):
        early_back(x)

    arrive(0)
    arrive(1)
    sum_finish(1, 0)
    sum_start(1, 1)
    for x in range(cx + 2 * HALO):
        inner = HALO <= x < cx + HALO
        for y in (0, 1, cy + 2, cy + 3) if inner else range(cy + 2 * HALO):
            put_delta(x, y)
    for x in range(2, cx):
        late_back(x)
    for x in (0, 1, cx, cx + 1):
        back(x)

    for x in range(cx):
        delta = s4[x + 1, chans : 2 * chans, depth : (1 + cy) * depth]
        grad(0, delta, s1, x + 1, 1)

    pack(0)
    sum_start(0, 0)
    sum_finish(1, 1)
    sum_start(1, 2)

    def last(x):
        total = conv(w1b_ref, s4, x, 0, cy + 2, cy, {})
        for y in range(cy):
            mask = flags(x + HALO, y + HALO)
            go[cell_rows(x, y), :] = jnp.where(mask > 0, total[y], 0.0)

    for x in range(cx):
        if x == cx // 2:
            sum_finish(0, 0)
            sum_start(0, 1)
        last(x)
    gin_ref[...] = go[...].reshape(chans, cx, cy, depth).astype(BF)

    sum_finish(1, 2)
    sum_start(1, 3)
    sum_finish(0, 1)
    sum_start(0, 2)
    sum_finish(1, 3)
    sum_finish(0, 2)
    sum_start(0, 3)
    sum_finish(0, 3)

    sent_f()
    for n in range(2):
        sent(n)
    for slot in range(2):
        for phase in range(4):
            for copy in sum_copies(slot, phase):
                copy.wait_send()


def publish_kernel(scale, chans, gin_ref, tot, gin_hbm, gw1, gb1, gw2, gb2, out, bias, sem):
    copies = [pltpu.make_async_copy(gin_ref, gin_hbm, sem.at[0])]
    copies[0].start()
    for slot, (weight_out, bias_out) in enumerate(((gw1, gb1), (gw2, gb2))):
        full = jnp.concatenate([tot[slot, 0], tot[slot, 1]], axis=0).astype(F32) * scale
        turned = jnp.concatenate([full, jnp.zeros((chans, full.shape[1]), F32)], axis=0).T
        for a in range(3):
            for b in range(3):
                for c in range(3):
                    n = a * 3 + c
                    row, column = (b, n) if n < 7 else (3, (n - 7) * 3 + b)
                    out[slot, a * 9 + b * 3 + c] = turned[
                        row * chans : (row + 1) * chans, column * chans : (column + 1) * chans
                    ]
        bias[slot] = full[6 * chans : 6 * chans + 1, 3 * chans : 4 * chans]
        for src, dst in ((out.at[slot], weight_out), (bias.at[slot], bias_out)):
            copies.append(pltpu.make_async_copy(src, dst, sem.at[len(copies)]))
            copies[-1].start()
    for copy in copies:
        copy.wait()


def body(features, occupancy, weight_one, bias_one, weight_two, bias_two, grad_pooled, pool_choice):
    chans, cx, cy, depth = features.shape
    nx, ny = lax.axis_size("gx"), lax.axis_size("gy")
    nz = nx // 2
    part = 7 * chans // 2
    bx, by, bz = occupancy.shape
    lanes = -(-(9 * chans + 1) // 128) * 128

    def taps_first(weight):
        return weight.transpose(1, 2, 3, 0, 4).reshape(27, chans, chans)

    def vm(shape, dtype):
        return pltpu.VMEM(shape, dtype)

    px, py, half = grad_pooled.shape[1:]
    hbm = pl.BlockSpec(memory_space=pltpu.HBM)
    vmem = pl.BlockSpec(memory_space=pltpu.VMEM)
    gin, tot = pl.pallas_call(
        functools.partial(main_kernel, nx, ny, cx, cy, depth, chans),
        out_shape=(
            jax.ShapeDtypeStruct(features.shape, BF),
            jax.ShapeDtypeStruct((2, 2, part, 4 * chans), BF),
        ),
        in_specs=[hbm] * 8,
        out_specs=(vmem,) * 2,
        scratch_shapes=[
            vm(features.shape, BF),
            vm(occupancy.shape, jnp.int32),
            vm((27, chans, chans), BF),
            vm((27, chans, chans), BF),
            vm((1, chans), F32),
            vm((1, chans), F32),
            vm(grad_pooled.shape, BF),
            vm(pool_choice.shape, jnp.int32),
            vm((chans * cx * cy, depth), F32),
            vm((chans * cx * cy, depth), F32),
            vm((2, chans * px * py, depth), F32),
            vm((lanes, 128), F32),
            vm((bx + 2, by + 2, depth), F32),
            vm((3 * chans, 9 * chans), BF),
            vm((3 * chans, 9 * chans), BF),
            vm((3 * chans, 9 * chans), BF),
            vm((3 * chans, 9 * chans), BF),
            vm((cx + 4, cy + 4, chans, depth), BF),
            vm((px + 2, py + 2, chans, depth), BF),
            vm((px + 2, py + 2, chans, depth), BF),
            vm((cx + 2, 4, chans, depth), F32),
            vm((cx, cy, chans, depth), F32),
            vm((cx + 4, 3 * chans, (cy + 4) * depth), BF),
            vm((cx + 2, 3 * chans, (cy + 2) * depth), BF),
            vm((cx + 4, 3 * chans, (cy + 4) * depth), BF),
            vm((cx + 2, 3 * chans, (cy + 2) * depth), BF),
            vm((2, 9 * chans + SPARE, 4 * chans), F32),
            vm((2, 2, part, 4 * chans), BF),
            vm((2, part, 4 * chans), BF),
            vm((2, ny, part, 4 * chans), BF),
            vm((2, nz, part, 4 * chans), BF),
            pltpu.SemaphoreType.DMA((8,)),
            pltpu.SemaphoreType.DMA((2 * (cx // HALO) + 6,)),
            pltpu.SemaphoreType.DMA((2 * (cx // HALO) + 6,)),
            pltpu.SemaphoreType.DMA((2, 8)),
            pltpu.SemaphoreType.DMA((2, 8)),
            pltpu.SemaphoreType.DMA((2, 4, max(ny, nz))),
            pltpu.SemaphoreType.DMA((2, 4, max(ny, nz))),
        ],
        compiler_params=pltpu.CompilerParams(
            collective_id=0, has_side_effects=True, vmem_limit_bytes=48 * 2**20
        ),
        name="main",
    )(*[pltpu.with_memory_space_constraint(v, pltpu.HBM) for v in (
        features, occupancy, taps_first(weight_one), taps_first(weight_two),
        bias_one.reshape(1, chans), bias_two.reshape(1, chans), grad_pooled, pool_choice,
    )])

    scale = 1.0 / math.sqrt(cx * nx * cy * ny * depth)
    taps = jax.ShapeDtypeStruct((27, chans, chans), F32)
    row = jax.ShapeDtypeStruct((1, chans), F32)
    gin, gw1, gb1, gw2, gb2 = pl.pallas_call(
        functools.partial(publish_kernel, scale, chans),
        out_shape=(jax.ShapeDtypeStruct(features.shape, BF), taps, row, taps, row),
        in_specs=[vmem] * 2,
        out_specs=(hbm,) * 5,
        scratch_shapes=[
            vm((2, 27, chans, chans), F32),
            vm((2, 1, chans), F32),
            pltpu.SemaphoreType.DMA((5,)),
        ],
        compiler_params=pltpu.CompilerParams(vmem_limit_bytes=8 * 2**20),
        name="publish",
    )(gin, tot)

    def taps_back(grads):
        return grads.reshape(3, 3, 3, chans, chans).transpose(3, 0, 1, 2, 4)

    return gin, taps_back(gw1), gb1.reshape(chans), taps_back(gw2), gb2.reshape(chans)


def solution(mesh):
    spread = P(None, "gx", "gy", None)
    return jax.shard_map(
        body,
        mesh=mesh,
        in_specs=(spread, P(), P(), P(), P(), P(), spread, spread),
        out_specs=(spread, P(), P(), P(), P()),
        check_vma=False,
    )
```

```python
import functools
import math

import jax
import jax.numpy as jnp
from jax import lax
from jax.experimental import pallas as pl
from jax.experimental.pallas import tpu as pltpu
from jax.sharding import PartitionSpec as P

MESH = pl.DeviceIdType.MESH
HALO = 2
SPARE = 16
SIDES = ((0, -1), (0, 1), (-1, -1), (-1, 1), (1, -1), (1, 1), (-1, 0), (1, 0))
BF = jnp.bfloat16
F32 = jnp.float32


def edge(side, cells, halo):
    if side == 0:
        return 0, cells
    return (0, halo) if side < 0 else (cells - halo, halo)


def landing(side, cells, halo):
    if side == 0:
        return halo
    return halo + cells if side < 0 else 0


def main_kernel(
    nx, ny, cx, cy, depth, chans,
    f_hbm, occ_hbm, w1_hbm, w2_hbm, b1_hbm, b2_hbm, gp_hbm, pc_hbm,
    gin_ref, tot,
    f_ref, occ_ref, wn1_ref, wn2_ref, b1_ref, b2_ref, gp_ref, pc_ref,
    ft, go, pt, wt, mz_ref, w1_ref, w2_ref, w1b_ref, w2b_ref,
    wide_f, wide_k, wide_w, part1, part2, s1, s2, s3, s4, gw_ref,
    gs, r0, q1, q2,
    held, edge_k, land_k, k_send, k_recv, local_sem, f_send, f_recv, relay_send, relay_recv, send_sem, recv_sem, sum_send, sum_recv,
):
    gx = lax.axis_index("gx")
    gy = lax.axis_index("gy")
    nz = nx // 2
    core = lax.rem(gx, 2)
    gz = gx // 2

    def exists(sx, sy):
        ok_x = jnp.logical_and(gx + sx >= 0, gx + sx < nx)
        ok_y = jnp.logical_and(gy + sy >= 0, gy + sy < ny)
        return jnp.logical_and(ok_x, ok_y)

    partner = (gx + 1 - 2 * core, gy)

    def peer_y(k):
        return (gx, lax.rem(gy + k, ny))

    def peer_z(k):
        return (2 * lax.rem(gz + k, nz) + core, gy)

    barrier = pltpu.get_barrier_semaphore()

    def greet(device):
        pl.semaphore_signal(barrier, inc=1, device_id=device, device_id_type=MESH)

    for k in range(1, nz):
        greet(peer_z(k))
    for k in range(1, ny):
        greet(peer_y(k))
    for sx, sy in SIDES:
        if sx:
            @pl.when(exists(sx, sy))
            def _():
                greet((gx + sx, gy + sy))
    beside_x = (gx > 0).astype(jnp.int32) + (gx < nx - 1).astype(jnp.int32)
    beside_y = (gy > 0).astype(jnp.int32) + (gy < ny - 1).astype(jnp.int32)

    local = [
        pltpu.make_async_copy(src, dst, local_sem.at[n])
        for n, (src, dst) in enumerate((
            (f_hbm, f_ref), (occ_hbm, occ_ref), (w1_hbm, wn1_ref), (w2_hbm, wn2_ref),
            (b1_hbm, b1_ref), (b2_hbm, b2_ref), (gp_hbm, gp_ref), (pc_hbm, pc_ref),
        ))
    ]
    for copy in local:
        copy.start()

    gw_ref[...] = jnp.zeros_like(gw_ref)

    mz_ref[...] = jnp.zeros_like(mz_ref)
    local[1].wait()
    bz = occ_ref.shape[2]
    repeat = (
        lax.broadcasted_iota(jnp.int32, (bz, depth), 1) // (depth // bz)
        == lax.broadcasted_iota(jnp.int32, (bz, depth), 0)
    ).astype(BF)
    for bx in range(occ_ref.shape[0]):
        row = occ_ref[bx].astype(F32).astype(BF)
        mz_ref[bx + 1, 1 : 1 + occ_ref.shape[1], :] = jnp.dot(
            row, repeat, preferred_element_type=F32
        )

    def cell_rows(x, y):
        return pl.ds(x * cy + y, chans, stride=cx * cy)

    local[0].wait()
    ft[...] = f_ref[...].astype(F32).reshape(chans * cx * cy, depth)
    for x in range(cx):
        for y in range(cy):
            wide_f[x + HALO, y + HALO] = ft[cell_rows(x, y), :].astype(BF)

    pl.semaphore_wait(barrier, nz - 1 + ny - 1 + beside_x + beside_x * beside_y)

    def copy_of(k):
        sx, sy = SIDES[k]
        ref, halo, wx, wy = wide_w, 1, cx // 2, cy // 2
        fx, lx = edge(sx, wx, halo)
        fy, ly = edge(sy, wy, halo)
        tx, ty = landing(sx, wx, halo), landing(sy, wy, halo)
        return pltpu.make_async_remote_copy(
            src_ref=ref.at[halo + fx : halo + fx + lx, halo + fy : halo + fy + ly],
            dst_ref=ref.at[tx : tx + lx, ty : ty + ly],
            send_sem=send_sem.at[k],
            recv_sem=recv_sem.at[k],
            device_id=(gx + sx, gy + sy),
            device_id_type=MESH,
        )

    def send():
        for far in (True, False) if ny == 4 else (False,):
            for k, (sx, sy) in enumerate(SIDES):
                ok = exists(sx, sy)
                if sy and ny == 4:
                    middle = is_source(sy)
                    ok = jnp.logical_and(ok, middle if far else jnp.logical_not(middle))
                elif far:
                    continue

                @pl.when(ok)
                def _():
                    copy_of(k).start()

    def arrive():
        for k, (sx, sy) in enumerate(SIDES):
            @pl.when(exists(-sx, -sy))
            def _():
                copy_of(k).wait_recv()

    def sent():
        for k, (sx, sy) in enumerate(SIDES):
            @pl.when(exists(sx, sy))
            def _():
                copy_of(k).wait_send()

    rows_apart = [HALO, cx] + list(range(2 * HALO, cx, HALO))

    def chunk(n, sy):
        fy = HALO if sy < 0 else cy
        ty = cy + HALO if sy < 0 else 0
        at = 2 * n + (sy > 0)
        x = rows_apart[n]
        return pltpu.make_async_remote_copy(
            src_ref=wide_f.at[x : x + HALO, fy : fy + HALO],
            dst_ref=wide_f.at[x : x + HALO, ty : ty + HALO],
            send_sem=f_send.at[at], recv_sem=f_recv.at[at],
            device_id=(gx, gy + sy), device_id_type=MESH,
        )

    def along_x(sx, sy):
        fx = HALO if sx < 0 else cx
        tx = cx + HALO if sx < 0 else 0
        y, count = (HALO, cy) if sy == 0 else (cy + HALO if sy < 0 else 0, HALO)
        at = 2 * len(rows_apart) + 2 * (sy % 3) + (sx > 0)
        return pltpu.make_async_remote_copy(
            src_ref=wide_f.at[fx : fx + HALO, y : y + count],
            dst_ref=wide_f.at[tx : tx + HALO, y : y + count],
            send_sem=f_send.at[at], recv_sem=f_recv.at[at],
            device_id=(gx + sx, gy), device_id_type=MESH,
        )

    relayed = range(2, len(rows_apart)) if ny == 4 else range(0)

    def is_source(sy):
        return gy == (1 if sy > 0 else 2)

    def is_relay(sy):
        return gy == (3 if sy > 0 else 0)

    def to_relay(n, sy):
        fy = HALO if sy < 0 else cy
        return pltpu.make_async_remote_copy(
            src_ref=wide_f.at[rows_apart[n] : rows_apart[n] + HALO, fy : fy + HALO],
            dst_ref=held.at[n - 2],
            send_sem=f_send.at[2 * n + (sy > 0)], recv_sem=relay_recv.at[n - 2],
            device_id=(gx, gy + 2 * sy), device_id_type=MESH,
        )

    def from_relay(n, sy):
        ty = cy + HALO if sy < 0 else 0
        return pltpu.make_async_remote_copy(
            src_ref=held.at[n - 2],
            dst_ref=wide_f.at[rows_apart[n] : rows_apart[n] + HALO, ty : ty + HALO],
            send_sem=relay_send.at[n - 2], recv_sem=f_recv.at[2 * n + (sy > 0)],
            device_id=(gx, gy - sy), device_id_type=MESH,
        )

    def pass_on(n):
        for sy in (-1, 1):
            @pl.when(is_relay(sy))
            def _():
                to_relay(n, sy).wait_recv()
                from_relay(n, sy).start()

    for n in relayed:
        for sy in (-1, 1):
            @pl.when(is_source(sy))
            def _():
                to_relay(n, sy).start()
    for n in range(len(rows_apart)):
        for sy in (-1, 1):
            direct = exists(0, sy)
            if n in relayed:
                direct = jnp.logical_and(direct, jnp.logical_not(is_source(sy)))

            @pl.when(direct)
            def _():
                chunk(n, sy).start()
        if n == 1:
            for sx in (-1, 1):
                @pl.when(exists(sx, 0))
                def _():
                    along_x(sx, 0).start()

    def take_chunk(n):
        for sy in (-1, 1):
            @pl.when(exists(0, -sy))
            def _():
                chunk(n, sy).wait_recv()
            for sx in (-1, 1):
                if n == (sx > 0):
                    @pl.when(exists(sx, -sy))
                    def _():
                        along_x(sx, sy).start()

    def take_x(sides):
        for sy in sides:
            for sx in (-1, 1):
                @pl.when(exists(-sx, -sy))
                def _():
                    along_x(sx, sy).wait_recv()

    def sent_f():
        for sy in (-1, 1):
            for n in range(len(rows_apart)):
                @pl.when(exists(0, sy))
                def _():
                    chunk(n, sy).wait_send()
                if n in relayed:
                    @pl.when(is_relay(sy))
                    def _():
                        from_relay(n, sy).wait_send()
        for sy in (0, -1, 1):
            for sx in (-1, 1):
                @pl.when(exists(sx, -sy))
                def _():
                    along_x(sx, sy).wait_send()

    for n, (nat, fwd, bwd) in enumerate(((wn1_ref, w1_ref, w1b_ref), (wn2_ref, w2_ref, w2b_ref))):
        local[2 + n].wait()
        wide = nat[...].astype(F32)
        for b in range(3):
            fwd[b * chans : (b + 1) * chans, :] = jnp.concatenate(
                [wide[a * 9 + b * 3 + c] for a in range(3) for c in range(3)], axis=1
            ).astype(BF)
        rows = wt.shape[0]
        wt[...] = jnp.zeros_like(wt)
        for a in range(3):
            for c in range(3):
                first = (a * 3 + c) * chans
                wt[first : first + chans, 0 : 3 * chans] = jnp.concatenate(
                    [wide[(2 - a) * 9 + (2 - b) * 3 + 2 - c] for b in range(3)], axis=1
                )
        turned = wt[...].T
        bwd[...] = turned[0 : 3 * chans, 0 : 9 * chans].astype(BF)

    half = depth // 2
    px, py = cx // 2, cy // 2
    spread = (
        lax.broadcasted_iota(jnp.int32, (half, depth), 1) // 2
        == lax.broadcasted_iota(jnp.int32, (half, depth), 0)
    ).astype(BF)
    local[6].wait()
    local[7].wait()
    for n, ref in enumerate((gp_ref, pc_ref)):
        for c in range(chans):
            for x in range(px):
                first = (c * px + x) * py
                pt[n, first : first + py, 0:half] = ref[c, x].astype(F32)
        if n:
            for side, y in enumerate((0, py - 1)):
                for x in range(0, px, 2):
                    pair = [pt[n, pl.ds((x + k) * py + y, chans, stride=px * py), :] for k in range(2)]
                    edge_k[side, x // 2] = jnp.concatenate(
                        [tile[:, 0:half] for tile in pair], axis=1
                    ).astype(BF)
        pt[n] = jnp.dot(pt[n, :, 0:half].astype(BF), spread, preferred_element_type=F32)

    def pooled(n, x, y):
        return pt[n, pl.ds(x * py + y, chans, stride=px * py), :]

    for x in range(px):
        for y in range(py):
            wide_k[x + 1, y + 1] = pooled(1, x, y).astype(BF)

    def choice_y(sy):
        side = int(sy > 0)
        return pltpu.make_async_remote_copy(
            src_ref=edge_k.at[side], dst_ref=land_k.at[side],
            send_sem=k_send.at[side], recv_sem=k_recv.at[side],
            device_id=(gx, gy + sy), device_id_type=MESH,
        )

    def choice_x(sx):
        side = int(sx > 0)
        return pltpu.make_async_remote_copy(
            src_ref=wide_k.at[px if sx > 0 else 1], dst_ref=wide_k.at[0 if sx > 0 else px + 1],
            send_sem=k_send.at[2 + side], recv_sem=k_recv.at[2 + side],
            device_id=(gx + sx, gy), device_id_type=MESH,
        )

    def choices_out():
        for sy in (-1, 1):
            @pl.when(exists(0, sy))
            def _():
                choice_y(sy).start()

    def choices_on():
        for sy in (-1, 1):
            @pl.when(exists(0, -sy))
            def _():
                choice_y(sy).wait_recv()
            twice = (
                lax.broadcasted_iota(jnp.int32, (depth, 2 * depth), 1) // 2
                == lax.broadcasted_iota(jnp.int32, (depth, 2 * depth), 0)
            ).astype(BF)
            for x in range(0, px, 2):
                both = jnp.dot(
                    land_k[int(sy > 0), x // 2], twice, preferred_element_type=F32
                ).astype(BF)
                for k in range(2):
                    wide_k[x + 1 + k, 0 if sy > 0 else py + 1] = both[:, lanes_of(k)]
        for sx in (-1, 1):
            @pl.when(exists(sx, 0))
            def _():
                choice_x(sx).start()

    def choices_in():
        for sx in (-1, 1):
            @pl.when(exists(-sx, 0))
            def _():
                choice_x(sx).wait_recv()

    def choices_sent():
        for side in (-1, 1):
            @pl.when(exists(0, side))
            def _():
                choice_y(side).wait_send()

            @pl.when(exists(side, 0))
            def _():
                choice_x(side).wait_send()

    same = lax.broadcasted_iota(jnp.int32, (chans, chans), 0) == lax.broadcasted_iota(
        jnp.int32, (chans, chans), 1
    )
    local[4].wait()
    local[5].wait()
    bias_one, bias_two = [
        jnp.sum(jnp.where(same, ref[...], 0.0), axis=1, keepdims=True) for ref in (b1_ref, b2_ref)
    ]
    lane = lax.broadcasted_iota(jnp.int32, (1, depth), 1)
    not_first = lane != 0
    not_last = lane != depth - 1
    lane_odd = lane % 2

    def flags(x, y):
        brick = gx * (cx // 8) + (x + 8 - HALO) // 8
        return mz_ref[brick, pl.ds(gy * (cy // 8) + (y + 8 - HALO) // 8, 1), :]

    def lanes_of(y, count=1):
        return slice(y * depth, (y + count) * depth)

    def put(stack, x, y, value):
        rounded = value.astype(BF)
        wide = rounded.astype(F32)
        where = lanes_of(y)
        stack[x, 0:chans, where] = jnp.where(not_first, pltpu.roll(wide, 1, 1), 0.0).astype(BF)
        stack[x, chans : 2 * chans, where] = rounded
        stack[x, 2 * chans : 3 * chans, where] = jnp.where(
            not_last, pltpu.roll(wide, depth - 1, 1), 0.0
        ).astype(BF)
        return rounded

    def put_cell(x, y):
        put(s1, x, y, jnp.where(flags(x, y) > 0, wide_f[x, y].astype(F32), 0.0))

    def conv(weight, stack, x, first, count, outs, total):
        rows = stack[pl.ds(x, 3), :, lanes_of(first, count)].reshape(9 * chans, count * depth)
        full = jnp.dot(weight[...], rows, preferred_element_type=F32)
        for t in range(count):
            for b in range(3):
                y = first + t - b
                if 0 <= y < outs:
                    piece = full[b * chans : (b + 1) * chans, lanes_of(t)]
                    total[y] = total[y] + piece if y in total else piece
        return total

    def grad(slot, delta, stack, x, first):
        width = (cy + 2) * depth
        rows = stack[pl.ds(x, 3), :, first * depth : first * depth + width].reshape(9 * chans, width)
        shifted = []
        for b in range(3):
            parts = []
            if b:
                parts.append(jnp.zeros((chans, b * depth), BF))
            parts.append(delta)
            if b < 2:
                parts.append(jnp.zeros((chans, (2 - b) * depth), BF))
            shifted.append(jnp.concatenate(parts, axis=1))
        left = jnp.concatenate(shifted, axis=0)
        right = jnp.concatenate([rows, jnp.ones((SPARE, width), BF)], axis=0)
        gw_ref[slot, :, 0 : 3 * chans] += lax.dot_general(
            right, left, (((1,), (1,)), ((), ())), preferred_element_type=F32
        )

    def pack(slot):
        total = gw_ref[slot]

        def block(n, b):
            return total[n * chans : (n + 1) * chans, b * chans : (b + 1) * chans]

        last = [block(n, b) for n in (7, 8) for b in range(3)]
        last.append(jnp.broadcast_to(total[9 * chans : 9 * chans + 1, 0:chans], (chans, chans)))
        full = jnp.concatenate(
            [
                jnp.concatenate([total[n * chans : (n + 1) * chans, 0 : 3 * chans], last[n]], axis=1)
                for n in range(7)
            ],
            axis=0,
        )
        gs[slot] = full.reshape(gs.shape[1:]).astype(BF)

    def sum_copies(slot, phase):
        if phase == 0:
            moves = [(gs.at[slot, 1 - core], r0.at[slot], partner)]
        elif phase == 1:
            moves = [(q1.at[slot, gy], q1.at[slot, gy], peer_y(k)) for k in range(1, ny)]
        elif phase == 2:
            moves = [(q2.at[slot, gz], q2.at[slot, gz], peer_z(k)) for k in range(1, nz)]
        else:
            moves = [(tot.at[slot, core], tot.at[slot, core], partner)]
        return [
            pltpu.make_async_remote_copy(
                src_ref=src, dst_ref=dst,
                send_sem=sum_send.at[slot, phase, k], recv_sem=sum_recv.at[slot, phase, k],
                device_id=device, device_id_type=MESH,
            )
            for k, (src, dst, device) in enumerate(moves)
        ]

    def sum_start(slot, phase):
        for copy in sum_copies(slot, phase):
            copy.start()

    def sum_finish(slot, phase):
        for copy in sum_copies(slot, phase):
            copy.wait_recv()
        if phase == 0:
            q1[slot, gy] = (gs[slot, core].astype(F32) + r0[slot].astype(F32)).astype(BF)
        if phase == 1:
            q2[slot, gz] = sum(q1[slot, k].astype(F32) for k in range(ny)).astype(BF)
        if phase == 2:
            tot[slot, core] = sum(q2[slot, k].astype(F32) for k in range(nz)).astype(BF)

    for x in range(cx):
        for y in range(cy):
            put_cell(x + HALO, y + HALO)

    def early_one(x):
        total = conv(w1_ref, s1, x, HALO, cy, cy + 2, {})
        for y in range(2, cy):
            hide(x, y, total[y])
        for n, y in enumerate((0, 1, cy, cy + 1)):
            part1[x, n] = total[y]

    def hide(x, y, pre):
        mask = flags(x + 1, y + 1)
        put(s2, x, y, jnp.where(mask > 0, jnp.maximum(pre + bias_one, 0.0), 0.0))

    for x in range(2, cx):
        early_one(x)
    for n in relayed[:1]:
        pass_on(n)
    take_x((0,))
    for n in relayed[1:]:
        pass_on(n)
    choices_out()
    for n in (0, 1, cx + 2, cx + 3):
        for y in range(cy):
            put_cell(n, y + HALO)
    for x in (0, 1, cx, cx + 1):
        early_one(x)

    def early_two(x):
        total = conv(w2_ref, s2, x, 2, cy - 2, cy, {})
        for y in range(cy):
            part2[x, y] = total[y]

    for x in range(cx):
        early_two(x)

    edges = (0, 1, cy, cy + 1)

    def late_one(x):
        total = {y: part1[x, n] for n, y in enumerate(edges)}
        conv(w1_ref, s1, x, 0, 2, cy + 2, total)
        conv(w1_ref, s1, x, cy + 2, 2, cy + 2, total)
        for y in edges:
            hide(x, y, total[y])

    def put_rows(x):
        for n in range(x, x + HALO):
            for y in (0, 1, cy + 2, cy + 3):
                put_cell(n, y)

    def choose(x):
        total = {y: part2[x, y] for y in range(cy)}
        conv(w2_ref, s2, x, 0, 2, cy, total)
        conv(w2_ref, s2, x, cy, 2, cy, total)
        out = []
        for y in range(cy):
            mask = flags(x + HALO, y + HALO)
            code = (4 * (x % 2) + 2 * (y % 2) + lane_odd).astype(F32)
            hit = jnp.where(pooled(1, x // 2, y // 2) == code, mask, 0.0)
            chosen = jnp.where(total[y] + bias_two > 0, hit, 0.0)
            delta = jnp.where(chosen > 0, pooled(0, x // 2, y // 2), 0.0)
            put(s3, x + HALO, y + HALO, delta)
            out.append(delta)
        return out

    def choose_pair(x):
        rows = [choose(2 * x), choose(2 * x + 1)]
        for y in range(py):
            cells = [row[2 * y + k] for row in rows for k in range(2)]
            wide_w[x + 1, y + 1] = sum(cells).astype(BF)

    ready = 2
    for n, x in enumerate(rows_apart):
        take_chunk(n)
        if n == 1:
            put_rows(rows_apart[0])
        if n:
            put_rows(x)
        if n == len(rows_apart) - 1:
            choices_on()
        if n > 1:
            last_row = cx if n == len(rows_apart) - 1 else x
            for row in range(ready, last_row):
                late_one(row)
            ready = last_row
    for x in range(1, px - 1):
        choose_pair(x)
    take_x((-1, 1))
    for x in (0, cx + HALO):
        put_rows(x)
    for x in (0, 1, cx, cx + 1):
        late_one(x)
    for x in (0, px - 1):
        choose_pair(x)

    send()

    for x in range(cx):
        delta = s3[x + HALO, chans : 2 * chans, HALO * depth : (HALO + cy) * depth]
        grad(1, delta, s2, x, 0)

    pack(1)
    sum_start(1, 0)

    def put_delta(x, y):
        code = (4 * (x % 2) + 2 * (y % 2) + lane_odd).astype(F32)
        hit = wide_k[x // 2, y // 2].astype(F32) == code
        value = jnp.where(hit, wide_w[x // 2, y // 2].astype(F32), 0.0)
        put(s3, x, y, jnp.where(flags(x, y) > 0, value, 0.0))

    def put_back(x, y, total):
        hidden = s2[x, chans : 2 * chans, lanes_of(y)].astype(F32)
        put(s4, x, y, jnp.where(hidden > 0, total, 0.0))

    def early_back(x):
        total = conv(w2b_ref, s3, x, HALO, cy, cy + 2, {})
        for y in range(2, cy):
            put_back(x, y, total[y])
        for n, y in enumerate(edges):
            part1[x, n] = total[y]

    def late_back(x):
        total = {y: part1[x, n] for n, y in enumerate(edges)}
        conv(w2b_ref, s3, x, 0, 2, cy + 2, total)
        conv(w2b_ref, s3, x, cy + 2, 2, cy + 2, total)
        for y in edges:
            put_back(x, y, total[y])

    def back(x):
        total = conv(w2b_ref, s3, x, 0, cy + 4, cy + 2, {})
        for y in range(cy + 2):
            put_back(x, y, total[y])

    for x in range(2, cx):
        early_back(x)

    sum_finish(1, 0)
    sum_start(1, 1)
    choices_in()
    arrive()
    for x in range(cx + 2 * HALO):
        inner = HALO <= x < cx + HALO
        for y in (0, 1, cy + 2, cy + 3) if inner else range(cy + 2 * HALO):
            put_delta(x, y)
    for x in range(2, cx):
        late_back(x)
    for x in (0, 1, cx, cx + 1):
        back(x)

    for x in range(cx):
        delta = s4[x + 1, chans : 2 * chans, depth : (1 + cy) * depth]
        grad(0, delta, s1, x + 1, 1)

    pack(0)
    sum_start(0, 0)

    def last(x):
        total = conv(w1b_ref, s4, x, 0, cy + 2, cy, {})
        for y in range(cy):
            mask = flags(x + HALO, y + HALO)
            go[cell_rows(x, y), :] = jnp.where(mask > 0, total[y], 0.0)

    for x in range(cx):
        if x == cx // 2:
            sum_finish(0, 0)
            sum_start(0, 1)
            sum_finish(1, 1)
            sum_start(1, 2)
        last(x)
    gin_ref[...] = go[...].reshape(chans, cx, cy, depth).astype(BF)

    sum_finish(0, 1)
    sum_start(0, 2)
    sum_finish(1, 2)
    sum_start(1, 3)
    sum_finish(0, 2)
    sum_start(0, 3)
    sum_finish(1, 3)
    sum_finish(0, 3)

    sent_f()
    choices_sent()
    sent()
    for slot in range(2):
        for phase in range(4):
            for copy in sum_copies(slot, phase):
                copy.wait_send()


def publish_kernel(scale, chans, gin_ref, tot, gin_hbm, gw1, gb1, gw2, gb2, out, bias, sem):
    copies = [pltpu.make_async_copy(gin_ref, gin_hbm, sem.at[0])]
    copies[0].start()
    for slot, (weight_out, bias_out) in enumerate(((gw1, gb1), (gw2, gb2))):
        full = jnp.concatenate([tot[slot, 0], tot[slot, 1]], axis=0).astype(F32) * scale
        turned = jnp.concatenate([full, jnp.zeros((chans, full.shape[1]), F32)], axis=0).T
        for a in range(3):
            for b in range(3):
                for c in range(3):
                    n = a * 3 + c
                    row, column = (b, n) if n < 7 else (3, (n - 7) * 3 + b)
                    out[slot, a * 9 + b * 3 + c] = turned[
                        row * chans : (row + 1) * chans, column * chans : (column + 1) * chans
                    ]
        bias[slot] = full[6 * chans : 6 * chans + 1, 3 * chans : 4 * chans]
        for src, dst in ((out.at[slot], weight_out), (bias.at[slot], bias_out)):
            copies.append(pltpu.make_async_copy(src, dst, sem.at[len(copies)]))
            copies[-1].start()
    for copy in copies:
        copy.wait()


def body(features, occupancy, weight_one, bias_one, weight_two, bias_two, grad_pooled, pool_choice):
    chans, cx, cy, depth = features.shape
    nx, ny = lax.axis_size("gx"), lax.axis_size("gy")
    nz = nx // 2
    part = 7 * chans // 2
    bx, by, bz = occupancy.shape
    lanes = -(-(9 * chans + 1) // 128) * 128

    def taps_first(weight):
        return weight.transpose(1, 2, 3, 0, 4).reshape(27, chans, chans)

    def vm(shape, dtype):
        return pltpu.VMEM(shape, dtype)

    px, py, half = grad_pooled.shape[1:]
    hbm = pl.BlockSpec(memory_space=pltpu.HBM)
    vmem = pl.BlockSpec(memory_space=pltpu.VMEM)
    gin, tot = pl.pallas_call(
        functools.partial(main_kernel, nx, ny, cx, cy, depth, chans),
        out_shape=(
            jax.ShapeDtypeStruct(features.shape, BF),
            jax.ShapeDtypeStruct((2, 2, part, 4 * chans), BF),
        ),
        in_specs=[hbm] * 8,
        out_specs=(vmem,) * 2,
        scratch_shapes=[
            vm(features.shape, BF),
            vm(occupancy.shape, jnp.int32),
            vm((27, chans, chans), BF),
            vm((27, chans, chans), BF),
            vm((1, chans), F32),
            vm((1, chans), F32),
            vm(grad_pooled.shape, BF),
            vm(pool_choice.shape, jnp.int32),
            vm((chans * cx * cy, depth), F32),
            vm((chans * cx * cy, depth), F32),
            vm((2, chans * px * py, depth), F32),
            vm((lanes, 128), F32),
            vm((bx + 2, by + 2, depth), F32),
            vm((3 * chans, 9 * chans), BF),
            vm((3 * chans, 9 * chans), BF),
            vm((3 * chans, 9 * chans), BF),
            vm((3 * chans, 9 * chans), BF),
            vm((cx + 4, cy + 4, chans, depth), BF),
            vm((px + 2, py + 2, chans, depth), BF),
            vm((px + 2, py + 2, chans, depth), BF),
            vm((cx + 2, 4, chans, depth), F32),
            vm((cx, cy, chans, depth), F32),
            vm((cx + 4, 3 * chans, (cy + 4) * depth), BF),
            vm((cx + 2, 3 * chans, (cy + 2) * depth), BF),
            vm((cx + 4, 3 * chans, (cy + 4) * depth), BF),
            vm((cx + 2, 3 * chans, (cy + 2) * depth), BF),
            vm((2, 9 * chans + SPARE, 4 * chans), F32),
            vm((2, 2, part, 4 * chans), BF),
            vm((2, part, 4 * chans), BF),
            vm((2, ny, part, 4 * chans), BF),
            vm((2, nz, part, 4 * chans), BF),
            vm((cx // HALO - 2, HALO, HALO, chans, depth), BF),
            vm((2, px // 2, chans, depth), BF),
            vm((2, px // 2, chans, depth), BF),
            pltpu.SemaphoreType.DMA((4,)),
            pltpu.SemaphoreType.DMA((4,)),
            pltpu.SemaphoreType.DMA((8,)),
            pltpu.SemaphoreType.DMA((2 * (cx // HALO) + 6,)),
            pltpu.SemaphoreType.DMA((2 * (cx // HALO) + 6,)),
            pltpu.SemaphoreType.DMA((cx // HALO - 2,)),
            pltpu.SemaphoreType.DMA((cx // HALO - 2,)),
            pltpu.SemaphoreType.DMA((8,)),
            pltpu.SemaphoreType.DMA((8,)),
            pltpu.SemaphoreType.DMA((2, 4, max(ny, nz))),
            pltpu.SemaphoreType.DMA((2, 4, max(ny, nz))),
        ],
        compiler_params=pltpu.CompilerParams(
            collective_id=0, has_side_effects=True, vmem_limit_bytes=48 * 2**20
        ),
        name="main",
    )(*[pltpu.with_memory_space_constraint(v, pltpu.HBM) for v in (
        features, occupancy, taps_first(weight_one), taps_first(weight_two),
        bias_one.reshape(1, chans), bias_two.reshape(1, chans), grad_pooled, pool_choice,
    )])

    scale = 1.0 / math.sqrt(cx * nx * cy * ny * depth)
    taps = jax.ShapeDtypeStruct((27, chans, chans), F32)
    row = jax.ShapeDtypeStruct((1, chans), F32)
    gin, gw1, gb1, gw2, gb2 = pl.pallas_call(
        functools.partial(publish_kernel, scale, chans),
        out_shape=(jax.ShapeDtypeStruct(features.shape, BF), taps, row, taps, row),
        in_specs=[vmem] * 2,
        out_specs=(hbm,) * 5,
        scratch_shapes=[
            vm((2, 27, chans, chans), F32),
            vm((2, 1, chans), F32),
            pltpu.SemaphoreType.DMA((5,)),
        ],
        compiler_params=pltpu.CompilerParams(vmem_limit_bytes=8 * 2**20),
        name="publish",
    )(gin, tot)

    def taps_back(grads):
        return grads.reshape(3, 3, 3, chans, chans).transpose(3, 0, 1, 2, 4)

    return gin, taps_back(gw1), gb1.reshape(chans), taps_back(gw2), gb2.reshape(chans)


def solution(mesh):
    spread = P(None, "gx", "gy", None)
    return jax.shard_map(
        body,
        mesh=mesh,
        in_specs=(spread, P(), P(), P(), P(), P(), spread, spread),
        out_specs=(spread, P(), P(), P(), P()),
        check_vma=False,
    )
```

```python
import functools
import math

import jax
import jax.numpy as jnp
from jax import lax
from jax.experimental import pallas as pl
from jax.experimental.pallas import tpu as pltpu
from jax.sharding import PartitionSpec as P

MESH = pl.DeviceIdType.MESH
HALO = 2
SPARE = 16
SIDES = ((0, -1), (0, 1), (-1, -1), (-1, 1), (1, -1), (1, 1), (-1, 0), (1, 0))
BF = jnp.bfloat16
F32 = jnp.float32


def edge(side, cells, halo):
    if side == 0:
        return 0, cells
    return (0, halo) if side < 0 else (cells - halo, halo)


def landing(side, cells, halo):
    if side == 0:
        return halo
    return halo + cells if side < 0 else 0


def main_kernel(
    nx, ny, cx, cy, depth, chans,
    f_hbm, occ_hbm, w1_hbm, w2_hbm, b1_hbm, b2_hbm, gp_hbm, pc_hbm,
    gin_ref, tot,
    f_ref, occ_ref, wn1_ref, wn2_ref, b1_ref, b2_ref, gp_ref, pc_ref,
    ft, go, pt, wt, mz_ref, w1_ref, w2_ref, w1b_ref, w2b_ref,
    wide_f, wide_k, wide_w, part1, part2, s1, s2, s3, s4, gw_ref,
    gs, r0, q1, q2,
    held, edge_k, land_k, k_send, k_recv, local_sem, f_send, f_recv, relay_send, relay_recv, send_sem, recv_sem, sum_send, sum_recv,
):
    gx = lax.axis_index("gx")
    gy = lax.axis_index("gy")
    nz = nx // 2
    core = lax.rem(gx, 2)
    gz = gx // 2

    def exists(sx, sy):
        ok_x = jnp.logical_and(gx + sx >= 0, gx + sx < nx)
        ok_y = jnp.logical_and(gy + sy >= 0, gy + sy < ny)
        return jnp.logical_and(ok_x, ok_y)

    partner = (gx + 1 - 2 * core, gy)

    def peer_y(k):
        return (gx, lax.rem(gy + k, ny))

    def peer_z(k):
        return (2 * lax.rem(gz + k, nz) + core, gy)

    barrier = pltpu.get_barrier_semaphore()

    def greet(device):
        pl.semaphore_signal(barrier, inc=1, device_id=device, device_id_type=MESH)

    for k in range(1, nz):
        greet(peer_z(k))
    for k in range(1, ny):
        greet(peer_y(k))
    for sx, sy in SIDES:
        if sx:
            @pl.when(exists(sx, sy))
            def _():
                greet((gx + sx, gy + sy))
    beside_x = (gx > 0).astype(jnp.int32) + (gx < nx - 1).astype(jnp.int32)
    beside_y = (gy > 0).astype(jnp.int32) + (gy < ny - 1).astype(jnp.int32)

    local = [
        pltpu.make_async_copy(src, dst, local_sem.at[n])
        for n, (src, dst) in enumerate((
            (f_hbm, f_ref), (occ_hbm, occ_ref), (w1_hbm, wn1_ref), (w2_hbm, wn2_ref),
            (b1_hbm, b1_ref), (b2_hbm, b2_ref), (gp_hbm, gp_ref), (pc_hbm, pc_ref),
        ))
    ]
    for copy in local:
        copy.start()

    gw_ref[...] = jnp.zeros_like(gw_ref)

    mz_ref[...] = jnp.zeros_like(mz_ref)
    local[1].wait()
    bz = occ_ref.shape[2]
    repeat = (
        lax.broadcasted_iota(jnp.int32, (bz, depth), 1) // (depth // bz)
        == lax.broadcasted_iota(jnp.int32, (bz, depth), 0)
    ).astype(BF)
    for bx in range(occ_ref.shape[0]):
        row = occ_ref[bx].astype(F32).astype(BF)
        mz_ref[bx + 1, 1 : 1 + occ_ref.shape[1], :] = jnp.dot(
            row, repeat, preferred_element_type=F32
        )

    def cell_rows(x, y):
        return pl.ds(x * cy + y, chans, stride=cx * cy)

    local[0].wait()
    ft[...] = f_ref[...].astype(F32).reshape(chans * cx * cy, depth)
    for x in range(cx):
        for y in range(cy):
            wide_f[x + HALO, y + HALO] = ft[cell_rows(x, y), :].astype(BF)

    pl.semaphore_wait(barrier, nz - 1 + ny - 1 + beside_x + beside_x * beside_y)

    pieces = []
    for sx, sy in SIDES:
        halves = ((0, cx // 2),)
        if sx == 0 and cx // 2 > 2:
            halves = ((1, cx // 2 - 2), (0, 1), (cx // 2 - 1, 1))
        pieces += [(sx, sy, first, count) for first, count in halves]

    def is_inner(k):
        return pieces[k][0] == 0 and pieces[k][2] == 1

    def copy_of(k):
        sx, sy, first, count = pieces[k]
        wx, wy = cx // 2, cy // 2
        fx, lx = edge(sx, wx, 1)
        fy, ly = edge(sy, wy, 1)
        tx, ty = landing(sx, wx, 1), landing(sy, wy, 1)
        if sx == 0:
            fx, lx, tx = first, count, 1 + first
        return pltpu.make_async_remote_copy(
            src_ref=wide_w.at[1 + fx : 1 + fx + lx, 1 + fy : 1 + fy + ly],
            dst_ref=wide_w.at[tx : tx + lx, ty : ty + ly],
            send_sem=send_sem.at[k],
            recv_sem=recv_sem.at[k],
            device_id=(gx + sx, gy + sy),
            device_id_type=MESH,
        )

    def send(inner):
        for far in (True, False) if ny == 4 else (False,):
            for k, (sx, sy, _, _) in enumerate(pieces):
                if is_inner(k) != inner:
                    continue
                ok = exists(sx, sy)
                if sy and ny == 4:
                    middle = is_source(sy)
                    ok = jnp.logical_and(ok, middle if far else jnp.logical_not(middle))
                elif far:
                    continue

                @pl.when(ok)
                def _():
                    copy_of(k).start()

    def arrive():
        for k, (sx, sy, _, _) in enumerate(pieces):
            @pl.when(exists(-sx, -sy))
            def _():
                copy_of(k).wait_recv()

    def sent():
        for k, (sx, sy, _, _) in enumerate(pieces):
            @pl.when(exists(sx, sy))
            def _():
                copy_of(k).wait_send()

    rows_apart = [HALO, cx] + list(range(2 * HALO, cx, HALO))

    def chunk(n, sy):
        fy = HALO if sy < 0 else cy
        ty = cy + HALO if sy < 0 else 0
        at = 2 * n + (sy > 0)
        x = rows_apart[n]
        return pltpu.make_async_remote_copy(
            src_ref=wide_f.at[x : x + HALO, fy : fy + HALO],
            dst_ref=wide_f.at[x : x + HALO, ty : ty + HALO],
            send_sem=f_send.at[at], recv_sem=f_recv.at[at],
            device_id=(gx, gy + sy), device_id_type=MESH,
        )

    def along_x(sx, sy):
        fx = HALO if sx < 0 else cx
        tx = cx + HALO if sx < 0 else 0
        y, count = (HALO, cy) if sy == 0 else (cy + HALO if sy < 0 else 0, HALO)
        at = 2 * len(rows_apart) + 2 * (sy % 3) + (sx > 0)
        return pltpu.make_async_remote_copy(
            src_ref=wide_f.at[fx : fx + HALO, y : y + count],
            dst_ref=wide_f.at[tx : tx + HALO, y : y + count],
            send_sem=f_send.at[at], recv_sem=f_recv.at[at],
            device_id=(gx + sx, gy), device_id_type=MESH,
        )

    relayed = range(2, len(rows_apart)) if ny == 4 else range(0)

    def is_source(sy):
        return gy == (1 if sy > 0 else 2)

    def is_relay(sy):
        return gy == (3 if sy > 0 else 0)

    def to_relay(n, sy):
        fy = HALO if sy < 0 else cy
        return pltpu.make_async_remote_copy(
            src_ref=wide_f.at[rows_apart[n] : rows_apart[n] + HALO, fy : fy + HALO],
            dst_ref=held.at[n - 2],
            send_sem=f_send.at[2 * n + (sy > 0)], recv_sem=relay_recv.at[n - 2],
            device_id=(gx, gy + 2 * sy), device_id_type=MESH,
        )

    def from_relay(n, sy):
        ty = cy + HALO if sy < 0 else 0
        return pltpu.make_async_remote_copy(
            src_ref=held.at[n - 2],
            dst_ref=wide_f.at[rows_apart[n] : rows_apart[n] + HALO, ty : ty + HALO],
            send_sem=relay_send.at[n - 2], recv_sem=f_recv.at[2 * n + (sy > 0)],
            device_id=(gx, gy - sy), device_id_type=MESH,
        )

    def pass_on(n):
        for sy in (-1, 1):
            @pl.when(is_relay(sy))
            def _():
                to_relay(n, sy).wait_recv()
                from_relay(n, sy).start()

    for n in relayed:
        for sy in (-1, 1):
            @pl.when(is_source(sy))
            def _():
                to_relay(n, sy).start()
    for n in range(len(rows_apart)):
        for sy in (-1, 1):
            direct = exists(0, sy)
            if n in relayed:
                direct = jnp.logical_and(direct, jnp.logical_not(is_source(sy)))

            @pl.when(direct)
            def _():
                chunk(n, sy).start()
        if n == 1:
            for sx in (-1, 1):
                @pl.when(exists(sx, 0))
                def _():
                    along_x(sx, 0).start()

    def take_chunk(n):
        for sy in (-1, 1):
            @pl.when(exists(0, -sy))
            def _():
                chunk(n, sy).wait_recv()
            for sx in (-1, 1):
                if n == (sx > 0):
                    @pl.when(exists(sx, -sy))
                    def _():
                        along_x(sx, sy).start()

    def take_x(sides):
        for sy in sides:
            for sx in (-1, 1):
                @pl.when(exists(-sx, -sy))
                def _():
                    along_x(sx, sy).wait_recv()

    def sent_f():
        for sy in (-1, 1):
            for n in range(len(rows_apart)):
                @pl.when(exists(0, sy))
                def _():
                    chunk(n, sy).wait_send()
                if n in relayed:
                    @pl.when(is_relay(sy))
                    def _():
                        from_relay(n, sy).wait_send()
        for sy in (0, -1, 1):
            for sx in (-1, 1):
                @pl.when(exists(sx, -sy))
                def _():
                    along_x(sx, sy).wait_send()

    for n, (nat, fwd, bwd) in enumerate(((wn1_ref, w1_ref, w1b_ref), (wn2_ref, w2_ref, w2b_ref))):
        local[2 + n].wait()
        wide = nat[...].astype(F32)
        for b in range(3):
            fwd[b * chans : (b + 1) * chans, :] = jnp.concatenate(
                [wide[a * 9 + b * 3 + c] for a in range(3) for c in range(3)], axis=1
            ).astype(BF)
        rows = wt.shape[0]
        wt[...] = jnp.zeros_like(wt)
        for a in range(3):
            for c in range(3):
                first = (a * 3 + c) * chans
                wt[first : first + chans, 0 : 3 * chans] = jnp.concatenate(
                    [wide[(2 - a) * 9 + (2 - b) * 3 + 2 - c] for b in range(3)], axis=1
                )
        turned = wt[...].T
        bwd[...] = turned[0 : 3 * chans, 0 : 9 * chans].astype(BF)

    half = depth // 2
    px, py = cx // 2, cy // 2
    spread = (
        lax.broadcasted_iota(jnp.int32, (half, depth), 1) // 2
        == lax.broadcasted_iota(jnp.int32, (half, depth), 0)
    ).astype(BF)
    local[6].wait()
    local[7].wait()
    for n, ref in enumerate((gp_ref, pc_ref)):
        for c in range(chans):
            for x in range(px):
                first = (c * px + x) * py
                pt[n, first : first + py, 0:half] = ref[c, x].astype(F32)
        if n:
            for side, y in enumerate((0, py - 1)):
                for x in range(0, px, 2):
                    pair = [pt[n, pl.ds((x + k) * py + y, chans, stride=px * py), :] for k in range(2)]
                    edge_k[side, x // 2] = jnp.concatenate(
                        [tile[:, 0:half] for tile in pair], axis=1
                    ).astype(BF)
        pt[n] = jnp.dot(pt[n, :, 0:half].astype(BF), spread, preferred_element_type=F32)

    def pooled(n, x, y):
        return pt[n, pl.ds(x * py + y, chans, stride=px * py), :]

    for x in range(px):
        for y in range(py):
            wide_k[x + 1, y + 1] = pooled(1, x, y).astype(BF)

    def choice_y(sy):
        side = int(sy > 0)
        return pltpu.make_async_remote_copy(
            src_ref=edge_k.at[side], dst_ref=land_k.at[side],
            send_sem=k_send.at[side], recv_sem=k_recv.at[side],
            device_id=(gx, gy + sy), device_id_type=MESH,
        )

    def choice_x(sx):
        side = int(sx > 0)
        return pltpu.make_async_remote_copy(
            src_ref=wide_k.at[px if sx > 0 else 1], dst_ref=wide_k.at[0 if sx > 0 else px + 1],
            send_sem=k_send.at[2 + side], recv_sem=k_recv.at[2 + side],
            device_id=(gx + sx, gy), device_id_type=MESH,
        )

    def choices_out():
        for sy in (-1, 1):
            @pl.when(exists(0, sy))
            def _():
                choice_y(sy).start()

    def choices_on():
        for sy in (-1, 1):
            @pl.when(exists(0, -sy))
            def _():
                choice_y(sy).wait_recv()
            twice = (
                lax.broadcasted_iota(jnp.int32, (depth, 2 * depth), 1) // 2
                == lax.broadcasted_iota(jnp.int32, (depth, 2 * depth), 0)
            ).astype(BF)
            for x in range(0, px, 2):
                both = jnp.dot(
                    land_k[int(sy > 0), x // 2], twice, preferred_element_type=F32
                ).astype(BF)
                for k in range(2):
                    wide_k[x + 1 + k, 0 if sy > 0 else py + 1] = both[:, lanes_of(k)]
        for sx in (-1, 1):
            @pl.when(exists(sx, 0))
            def _():
                choice_x(sx).start()

    def choices_in():
        for sx in (-1, 1):
            @pl.when(exists(-sx, 0))
            def _():
                choice_x(sx).wait_recv()

    def choices_sent():
        for side in (-1, 1):
            @pl.when(exists(0, side))
            def _():
                choice_y(side).wait_send()

            @pl.when(exists(side, 0))
            def _():
                choice_x(side).wait_send()

    same = lax.broadcasted_iota(jnp.int32, (chans, chans), 0) == lax.broadcasted_iota(
        jnp.int32, (chans, chans), 1
    )
    local[4].wait()
    local[5].wait()
    bias_one, bias_two = [
        jnp.sum(jnp.where(same, ref[...], 0.0), axis=1, keepdims=True) for ref in (b1_ref, b2_ref)
    ]
    lane = lax.broadcasted_iota(jnp.int32, (1, depth), 1)
    not_first = lane != 0
    not_last = lane != depth - 1
    lane_odd = lane % 2

    def flags(x, y):
        brick = gx * (cx // 8) + (x + 8 - HALO) // 8
        return mz_ref[brick, pl.ds(gy * (cy // 8) + (y + 8 - HALO) // 8, 1), :]

    def lanes_of(y, count=1):
        return slice(y * depth, (y + count) * depth)

    def put(stack, x, y, value):
        rounded = value.astype(BF)
        wide = rounded.astype(F32)
        where = lanes_of(y)
        stack[x, 0:chans, where] = jnp.where(not_first, pltpu.roll(wide, 1, 1), 0.0).astype(BF)
        stack[x, chans : 2 * chans, where] = rounded
        stack[x, 2 * chans : 3 * chans, where] = jnp.where(
            not_last, pltpu.roll(wide, depth - 1, 1), 0.0
        ).astype(BF)
        return rounded

    def put_cell(x, y):
        put(s1, x, y, jnp.where(flags(x, y) > 0, wide_f[x, y].astype(F32), 0.0))

    def conv(weight, stack, x, first, count, outs, total):
        rows = stack[pl.ds(x, 3), :, lanes_of(first, count)].reshape(9 * chans, count * depth)
        full = jnp.dot(weight[...], rows, preferred_element_type=F32)
        for t in range(count):
            for b in range(3):
                y = first + t - b
                if 0 <= y < outs:
                    piece = full[b * chans : (b + 1) * chans, lanes_of(t)]
                    total[y] = total[y] + piece if y in total else piece
        return total

    def grad(slot, delta, stack, x, first):
        width = (cy + 2) * depth
        rows = stack[pl.ds(x, 3), :, first * depth : first * depth + width].reshape(9 * chans, width)
        shifted = []
        for b in range(3):
            parts = []
            if b:
                parts.append(jnp.zeros((chans, b * depth), BF))
            parts.append(delta)
            if b < 2:
                parts.append(jnp.zeros((chans, (2 - b) * depth), BF))
            shifted.append(jnp.concatenate(parts, axis=1))
        left = jnp.concatenate(shifted, axis=0)
        right = jnp.concatenate([rows, jnp.ones((SPARE, width), BF)], axis=0)
        gw_ref[slot, :, 0 : 3 * chans] += lax.dot_general(
            right, left, (((1,), (1,)), ((), ())), preferred_element_type=F32
        )

    def pack(slot):
        total = gw_ref[slot]

        def block(n, b):
            return total[n * chans : (n + 1) * chans, b * chans : (b + 1) * chans]

        last = [block(n, b) for n in (7, 8) for b in range(3)]
        last.append(jnp.broadcast_to(total[9 * chans : 9 * chans + 1, 0:chans], (chans, chans)))
        full = jnp.concatenate(
            [
                jnp.concatenate([total[n * chans : (n + 1) * chans, 0 : 3 * chans], last[n]], axis=1)
                for n in range(7)
            ],
            axis=0,
        )
        gs[slot] = full.reshape(gs.shape[1:]).astype(BF)

    def sum_copies(slot, phase):
        if phase == 0:
            moves = [(gs.at[slot, 1 - core], r0.at[slot], partner)]
        elif phase == 1:
            moves = [(q1.at[slot, gy], q1.at[slot, gy], peer_y(k)) for k in range(1, ny)]
        elif phase == 2:
            moves = [(q2.at[slot, gz], q2.at[slot, gz], peer_z(k)) for k in range(1, nz)]
        else:
            moves = [(tot.at[slot, core], tot.at[slot, core], partner)]
        return [
            pltpu.make_async_remote_copy(
                src_ref=src, dst_ref=dst,
                send_sem=sum_send.at[slot, phase, k], recv_sem=sum_recv.at[slot, phase, k],
                device_id=device, device_id_type=MESH,
            )
            for k, (src, dst, device) in enumerate(moves)
        ]

    def sum_start(slot, phase):
        for copy in sum_copies(slot, phase):
            copy.start()

    def sum_finish(slot, phase):
        for copy in sum_copies(slot, phase):
            copy.wait_recv()
        if phase == 0:
            q1[slot, gy] = (gs[slot, core].astype(F32) + r0[slot].astype(F32)).astype(BF)
        if phase == 1:
            q2[slot, gz] = sum(q1[slot, k].astype(F32) for k in range(ny)).astype(BF)
        if phase == 2:
            tot[slot, core] = sum(q2[slot, k].astype(F32) for k in range(nz)).astype(BF)

    for x in range(cx):
        for y in range(cy):
            put_cell(x + HALO, y + HALO)

    def early_one(x):
        total = conv(w1_ref, s1, x, HALO, cy, cy + 2, {})
        for y in range(2, cy):
            hide(x, y, total[y])
        for n, y in enumerate((0, 1, cy, cy + 1)):
            part1[x, n] = total[y]

    def hide(x, y, pre):
        mask = flags(x + 1, y + 1)
        put(s2, x, y, jnp.where(mask > 0, jnp.maximum(pre + bias_one, 0.0), 0.0))

    for x in range(2, cx):
        early_one(x)
    for n in relayed[:1]:
        pass_on(n)
    take_x((0,))
    for n in relayed[1:]:
        pass_on(n)
    choices_out()
    for n in (0, 1, cx + 2, cx + 3):
        for y in range(cy):
            put_cell(n, y + HALO)
    for x in (0, 1, cx, cx + 1):
        early_one(x)

    def early_two(x):
        total = conv(w2_ref, s2, x, 2, cy - 2, cy, {})
        for y in range(cy):
            part2[x, y] = total[y]

    for x in range(cx):
        early_two(x)

    edges = (0, 1, cy, cy + 1)

    def late_one(x):
        total = {y: part1[x, n] for n, y in enumerate(edges)}
        conv(w1_ref, s1, x, 0, 2, cy + 2, total)
        conv(w1_ref, s1, x, cy + 2, 2, cy + 2, total)
        for y in edges:
            hide(x, y, total[y])

    def put_rows(x):
        for n in range(x, x + HALO):
            for y in (0, 1, cy + 2, cy + 3):
                put_cell(n, y)

    def choose(x):
        total = {y: part2[x, y] for y in range(cy)}
        conv(w2_ref, s2, x, 0, 2, cy, total)
        conv(w2_ref, s2, x, cy, 2, cy, total)
        out = []
        for y in range(cy):
            mask = flags(x + HALO, y + HALO)
            code = (4 * (x % 2) + 2 * (y % 2) + lane_odd).astype(F32)
            hit = jnp.where(pooled(1, x // 2, y // 2) == code, mask, 0.0)
            chosen = jnp.where(total[y] + bias_two > 0, hit, 0.0)
            delta = jnp.where(chosen > 0, pooled(0, x // 2, y // 2), 0.0)
            put(s3, x + HALO, y + HALO, delta)
            out.append(delta)
        return out

    def choose_pair(x):
        rows = [choose(2 * x), choose(2 * x + 1)]
        for y in range(py):
            cells = [row[2 * y + k] for row in rows for k in range(2)]
            wide_w[x + 1, y + 1] = sum(cells).astype(BF)

    ready = 2
    for n, x in enumerate(rows_apart):
        take_chunk(n)
        if n == 1:
            put_rows(rows_apart[0])
        if n:
            put_rows(x)
        if n == len(rows_apart) - 1:
            choices_on()
        if n > 1:
            last_row = cx if n == len(rows_apart) - 1 else x
            for row in range(ready, last_row):
                late_one(row)
            ready = last_row
    for x in range(1, px - 1):
        choose_pair(x)
    send(True)
    take_x((-1, 1))
    for x in (0, cx + HALO):
        put_rows(x)
    for x in (0, 1, cx, cx + 1):
        late_one(x)
    for x in (0, px - 1):
        choose_pair(x)

    send(False)

    for x in range(cx):
        delta = s3[x + HALO, chans : 2 * chans, HALO * depth : (HALO + cy) * depth]
        grad(1, delta, s2, x, 0)

    pack(1)
    sum_start(1, 0)

    def put_delta(x, y):
        code = (4 * (x % 2) + 2 * (y % 2) + lane_odd).astype(F32)
        hit = wide_k[x // 2, y // 2].astype(F32) == code
        value = jnp.where(hit, wide_w[x // 2, y // 2].astype(F32), 0.0)
        put(s3, x, y, jnp.where(flags(x, y) > 0, value, 0.0))

    def put_back(x, y, total):
        hidden = s2[x, chans : 2 * chans, lanes_of(y)].astype(F32)
        put(s4, x, y, jnp.where(hidden > 0, total, 0.0))

    def early_back(x):
        total = conv(w2b_ref, s3, x, HALO, cy, cy + 2, {})
        for y in range(2, cy):
            put_back(x, y, total[y])
        for n, y in enumerate(edges):
            part1[x, n] = total[y]

    def late_back(x):
        total = {y: part1[x, n] for n, y in enumerate(edges)}
        conv(w2b_ref, s3, x, 0, 2, cy + 2, total)
        conv(w2b_ref, s3, x, cy + 2, 2, cy + 2, total)
        for y in edges:
            put_back(x, y, total[y])

    def back(x):
        total = conv(w2b_ref, s3, x, 0, cy + 4, cy + 2, {})
        for y in range(cy + 2):
            put_back(x, y, total[y])

    for x in range(2, cx):
        early_back(x)

    sum_finish(1, 0)
    sum_start(1, 1)
    choices_in()
    arrive()
    for x in range(cx + 2 * HALO):
        inner = HALO <= x < cx + HALO
        for y in (0, 1, cy + 2, cy + 3) if inner else range(cy + 2 * HALO):
            put_delta(x, y)
    for x in range(2, cx):
        late_back(x)
    for x in (0, 1, cx, cx + 1):
        back(x)

    for x in range(cx):
        delta = s4[x + 1, chans : 2 * chans, depth : (1 + cy) * depth]
        grad(0, delta, s1, x + 1, 1)

    pack(0)
    sum_start(0, 0)

    def last(x):
        total = conv(w1b_ref, s4, x, 0, cy + 2, cy, {})
        for y in range(cy):
            mask = flags(x + HALO, y + HALO)
            go[cell_rows(x, y), :] = jnp.where(mask > 0, total[y], 0.0)

    for x in range(cx):
        if x == cx // 2:
            sum_finish(0, 0)
            sum_start(0, 1)
            sum_finish(1, 1)
            sum_start(1, 2)
        last(x)
    gin_ref[...] = go[...].reshape(chans, cx, cy, depth).astype(BF)

    sum_finish(0, 1)
    sum_start(0, 2)
    sum_finish(1, 2)
    sum_start(1, 3)
    sum_finish(0, 2)
    sum_start(0, 3)
    sum_finish(1, 3)
    sum_finish(0, 3)

    sent_f()
    choices_sent()
    sent()
    for slot in range(2):
        for phase in range(4):
            for copy in sum_copies(slot, phase):
                copy.wait_send()


def publish_kernel(scale, chans, gin_ref, tot, gin_hbm, gw1, gb1, gw2, gb2, out, bias, sem):
    copies = [pltpu.make_async_copy(gin_ref, gin_hbm, sem.at[0])]
    copies[0].start()
    for slot, (weight_out, bias_out) in enumerate(((gw1, gb1), (gw2, gb2))):
        full = jnp.concatenate([tot[slot, 0], tot[slot, 1]], axis=0).astype(F32) * scale
        turned = jnp.concatenate([full, jnp.zeros((chans, full.shape[1]), F32)], axis=0).T
        for a in range(3):
            for b in range(3):
                for c in range(3):
                    n = a * 3 + c
                    row, column = (b, n) if n < 7 else (3, (n - 7) * 3 + b)
                    out[slot, a * 9 + b * 3 + c] = turned[
                        row * chans : (row + 1) * chans, column * chans : (column + 1) * chans
                    ]
        bias[slot] = full[6 * chans : 6 * chans + 1, 3 * chans : 4 * chans]
        for src, dst in ((out.at[slot], weight_out), (bias.at[slot], bias_out)):
            copies.append(pltpu.make_async_copy(src, dst, sem.at[len(copies)]))
            copies[-1].start()
    for copy in copies:
        copy.wait()


def body(features, occupancy, weight_one, bias_one, weight_two, bias_two, grad_pooled, pool_choice):
    chans, cx, cy, depth = features.shape
    nx, ny = lax.axis_size("gx"), lax.axis_size("gy")
    nz = nx // 2
    part = 7 * chans // 2
    bx, by, bz = occupancy.shape
    lanes = -(-(9 * chans + 1) // 128) * 128

    def taps_first(weight):
        return weight.transpose(1, 2, 3, 0, 4).reshape(27, chans, chans)

    def vm(shape, dtype):
        return pltpu.VMEM(shape, dtype)

    px, py, half = grad_pooled.shape[1:]
    hbm = pl.BlockSpec(memory_space=pltpu.HBM)
    vmem = pl.BlockSpec(memory_space=pltpu.VMEM)
    gin, tot = pl.pallas_call(
        functools.partial(main_kernel, nx, ny, cx, cy, depth, chans),
        out_shape=(
            jax.ShapeDtypeStruct(features.shape, BF),
            jax.ShapeDtypeStruct((2, 2, part, 4 * chans), BF),
        ),
        in_specs=[hbm] * 8,
        out_specs=(vmem,) * 2,
        scratch_shapes=[
            vm(features.shape, BF),
            vm(occupancy.shape, jnp.int32),
            vm((27, chans, chans), BF),
            vm((27, chans, chans), BF),
            vm((1, chans), F32),
            vm((1, chans), F32),
            vm(grad_pooled.shape, BF),
            vm(pool_choice.shape, jnp.int32),
            vm((chans * cx * cy, depth), F32),
            vm((chans * cx * cy, depth), F32),
            vm((2, chans * px * py, depth), F32),
            vm((lanes, 128), F32),
            vm((bx + 2, by + 2, depth), F32),
            vm((3 * chans, 9 * chans), BF),
            vm((3 * chans, 9 * chans), BF),
            vm((3 * chans, 9 * chans), BF),
            vm((3 * chans, 9 * chans), BF),
            vm((cx + 4, cy + 4, chans, depth), BF),
            vm((px + 2, py + 2, chans, depth), BF),
            vm((px + 2, py + 2, chans, depth), BF),
            vm((cx + 2, 4, chans, depth), F32),
            vm((cx, cy, chans, depth), F32),
            vm((cx + 4, 3 * chans, (cy + 4) * depth), BF),
            vm((cx + 2, 3 * chans, (cy + 2) * depth), BF),
            vm((cx + 4, 3 * chans, (cy + 4) * depth), BF),
            vm((cx + 2, 3 * chans, (cy + 2) * depth), BF),
            vm((2, 9 * chans + SPARE, 4 * chans), F32),
            vm((2, 2, part, 4 * chans), BF),
            vm((2, part, 4 * chans), BF),
            vm((2, ny, part, 4 * chans), BF),
            vm((2, nz, part, 4 * chans), BF),
            vm((cx // HALO - 2, HALO, HALO, chans, depth), BF),
            vm((2, px // 2, chans, depth), BF),
            vm((2, px // 2, chans, depth), BF),
            pltpu.SemaphoreType.DMA((4,)),
            pltpu.SemaphoreType.DMA((4,)),
            pltpu.SemaphoreType.DMA((8,)),
            pltpu.SemaphoreType.DMA((2 * (cx // HALO) + 6,)),
            pltpu.SemaphoreType.DMA((2 * (cx // HALO) + 6,)),
            pltpu.SemaphoreType.DMA((cx // HALO - 2,)),
            pltpu.SemaphoreType.DMA((cx // HALO - 2,)),
            pltpu.SemaphoreType.DMA((12,)),
            pltpu.SemaphoreType.DMA((12,)),
            pltpu.SemaphoreType.DMA((2, 4, max(ny, nz))),
            pltpu.SemaphoreType.DMA((2, 4, max(ny, nz))),
        ],
        compiler_params=pltpu.CompilerParams(
            collective_id=0, has_side_effects=True, vmem_limit_bytes=48 * 2**20
        ),
        name="main",
    )(*[pltpu.with_memory_space_constraint(v, pltpu.HBM) for v in (
        features, occupancy, taps_first(weight_one), taps_first(weight_two),
        bias_one.reshape(1, chans), bias_two.reshape(1, chans), grad_pooled, pool_choice,
    )])

    scale = 1.0 / math.sqrt(cx * nx * cy * ny * depth)
    taps = jax.ShapeDtypeStruct((27, chans, chans), F32)
    row = jax.ShapeDtypeStruct((1, chans), F32)
    gin, gw1, gb1, gw2, gb2 = pl.pallas_call(
        functools.partial(publish_kernel, scale, chans),
        out_shape=(jax.ShapeDtypeStruct(features.shape, BF), taps, row, taps, row),
        in_specs=[vmem] * 2,
        out_specs=(hbm,) * 5,
        scratch_shapes=[
            vm((2, 27, chans, chans), F32),
            vm((2, 1, chans), F32),
            pltpu.SemaphoreType.DMA((5,)),
        ],
        compiler_params=pltpu.CompilerParams(vmem_limit_bytes=8 * 2**20),
        name="publish",
    )(gin, tot)

    def taps_back(grads):
        return grads.reshape(3, 3, 3, chans, chans).transpose(3, 0, 1, 2, 4)

    return gin, taps_back(gw1), gb1.reshape(chans), taps_back(gw2), gb2.reshape(chans)


def solution(mesh):
    spread = P(None, "gx", "gy", None)
    return jax.shard_map(
        body,
        mesh=mesh,
        in_specs=(spread, P(), P(), P(), P(), P(), spread, spread),
        out_specs=(spread, P(), P(), P(), P()),
        check_vma=False,
    )
```

```python
import functools
import math

import jax
import jax.numpy as jnp
from jax import lax
from jax.experimental import pallas as pl
from jax.experimental.pallas import tpu as pltpu
from jax.sharding import PartitionSpec as P

MESH = pl.DeviceIdType.MESH
HALO = 2
SPARE = 16
SIDES = ((0, -1), (0, 1), (-1, -1), (-1, 1), (1, -1), (1, 1), (-1, 0), (1, 0))
BF = jnp.bfloat16
F32 = jnp.float32


def edge(side, cells, halo):
    if side == 0:
        return 0, cells
    return (0, halo) if side < 0 else (cells - halo, halo)


def landing(side, cells, halo):
    if side == 0:
        return halo
    return halo + cells if side < 0 else 0


def main_kernel(
    nx, ny, cx, cy, depth, chans,
    f_hbm, occ_hbm, w1_hbm, w2_hbm, b1_hbm, b2_hbm, gp_hbm, pc_hbm,
    gin_ref, tot,
    f_ref, occ_ref, wn1_ref, wn2_ref, b1_ref, b2_ref, gp_ref, pc_ref,
    ft, go, pt, wt, mz_ref, w1_ref, w2_ref, w1b_ref, w2b_ref,
    wide_f, wide_k, wide_w, part1, part2, s1, s2, s3, s4, gw_ref,
    gs, r0, q1, q2,
    held, edge_k, land_k, k_send, k_recv, local_sem, f_send, f_recv, relay_send, relay_recv, send_sem, recv_sem, sum_send, sum_recv,
):
    gx = lax.axis_index("gx")
    gy = lax.axis_index("gy")
    nz = nx // 2
    core = lax.rem(gx, 2)
    gz = gx // 2

    def exists(sx, sy):
        ok_x = jnp.logical_and(gx + sx >= 0, gx + sx < nx)
        ok_y = jnp.logical_and(gy + sy >= 0, gy + sy < ny)
        return jnp.logical_and(ok_x, ok_y)

    partner = (gx + 1 - 2 * core, gy)

    def peer_y(k):
        return (gx, lax.rem(gy + k, ny))

    def peer_z(k):
        return (2 * lax.rem(gz + k, nz) + core, gy)

    barrier = pltpu.get_barrier_semaphore()

    def greet(device):
        pl.semaphore_signal(barrier, inc=1, device_id=device, device_id_type=MESH)

    for k in range(1, nz):
        greet(peer_z(k))
    for k in range(1, ny):
        greet(peer_y(k))
    for sx, sy in SIDES:
        if sx:
            @pl.when(exists(sx, sy))
            def _():
                greet((gx + sx, gy + sy))
    beside_x = (gx > 0).astype(jnp.int32) + (gx < nx - 1).astype(jnp.int32)
    beside_y = (gy > 0).astype(jnp.int32) + (gy < ny - 1).astype(jnp.int32)

    local = [
        pltpu.make_async_copy(src, dst, local_sem.at[n])
        for n, (src, dst) in enumerate((
            (f_hbm, f_ref), (occ_hbm, occ_ref), (w1_hbm, wn1_ref), (w2_hbm, wn2_ref),
            (b1_hbm, b1_ref), (b2_hbm, b2_ref), (gp_hbm, gp_ref), (pc_hbm, pc_ref),
        ))
    ]
    for copy in local:
        copy.start()

    gw_ref[...] = jnp.zeros_like(gw_ref)

    mz_ref[...] = jnp.zeros_like(mz_ref)
    local[1].wait()
    bz = occ_ref.shape[2]
    repeat = (
        lax.broadcasted_iota(jnp.int32, (bz, depth), 1) // (depth // bz)
        == lax.broadcasted_iota(jnp.int32, (bz, depth), 0)
    ).astype(BF)
    for bx in range(occ_ref.shape[0]):
        row = occ_ref[bx].astype(F32).astype(BF)
        mz_ref[bx + 1, 1 : 1 + occ_ref.shape[1], :] = jnp.dot(
            row, repeat, preferred_element_type=F32
        )

    def cell_rows(x, y):
        return pl.ds(x * cy + y, chans, stride=cx * cy)

    local[0].wait()
    ft[...] = f_ref[...].astype(F32).reshape(chans * cx * cy, depth)
    for x in range(cx):
        for y in range(cy):
            wide_f[x + HALO, y + HALO] = ft[cell_rows(x, y), :].astype(BF)

    pl.semaphore_wait(barrier, nz - 1 + ny - 1 + beside_x + beside_x * beside_y)

    pieces = []
    for sx, sy in SIDES:
        halves = ((0, cx // 2),)
        if sx == 0 and cx // 2 > 2:
            halves = ((1, cx // 2 - 2), (0, 1), (cx // 2 - 1, 1))
        pieces += [(sx, sy, first, count) for first, count in halves]

    def is_inner(k):
        return pieces[k][0] == 0 and pieces[k][2] == 1

    def copy_of(k):
        sx, sy, first, count = pieces[k]
        wx, wy = cx // 2, cy // 2
        fx, lx = edge(sx, wx, 1)
        fy, ly = edge(sy, wy, 1)
        tx, ty = landing(sx, wx, 1), landing(sy, wy, 1)
        if sx == 0:
            fx, lx, tx = first, count, 1 + first
        return pltpu.make_async_remote_copy(
            src_ref=wide_w.at[1 + fx : 1 + fx + lx, 1 + fy : 1 + fy + ly],
            dst_ref=wide_w.at[tx : tx + lx, ty : ty + ly],
            send_sem=send_sem.at[k],
            recv_sem=recv_sem.at[k],
            device_id=(gx + sx, gy + sy),
            device_id_type=MESH,
        )

    def send(inner):
        for far in (True, False) if ny == 4 else (False,):
            for k, (sx, sy, _, _) in enumerate(pieces):
                if is_inner(k) != inner:
                    continue
                ok = exists(sx, sy)
                if sy and ny == 4:
                    middle = is_source(sy)
                    ok = jnp.logical_and(ok, middle if far else jnp.logical_not(middle))
                elif far:
                    continue

                @pl.when(ok)
                def _():
                    copy_of(k).start()

    def arrive():
        for k, (sx, sy, _, _) in enumerate(pieces):
            @pl.when(exists(-sx, -sy))
            def _():
                copy_of(k).wait_recv()

    def sent():
        for k, (sx, sy, _, _) in enumerate(pieces):
            @pl.when(exists(sx, sy))
            def _():
                copy_of(k).wait_send()

    rows_apart = [HALO, cx] + list(range(2 * HALO, cx, HALO))

    def chunk(n, sy):
        fy = HALO if sy < 0 else cy
        ty = cy + HALO if sy < 0 else 0
        at = 2 * n + (sy > 0)
        x = rows_apart[n]
        return pltpu.make_async_remote_copy(
            src_ref=wide_f.at[x : x + HALO, fy : fy + HALO],
            dst_ref=wide_f.at[x : x + HALO, ty : ty + HALO],
            send_sem=f_send.at[at], recv_sem=f_recv.at[at],
            device_id=(gx, gy + sy), device_id_type=MESH,
        )

    def along_x(sx, sy):
        fx = HALO if sx < 0 else cx
        tx = cx + HALO if sx < 0 else 0
        y, count = (HALO, cy) if sy == 0 else (cy + HALO if sy < 0 else 0, HALO)
        at = 2 * len(rows_apart) + 2 * (sy % 3) + (sx > 0)
        return pltpu.make_async_remote_copy(
            src_ref=wide_f.at[fx : fx + HALO, y : y + count],
            dst_ref=wide_f.at[tx : tx + HALO, y : y + count],
            send_sem=f_send.at[at], recv_sem=f_recv.at[at],
            device_id=(gx + sx, gy), device_id_type=MESH,
        )

    relayed = range(2, len(rows_apart)) if ny == 4 else range(0)

    def is_source(sy):
        return gy == (1 if sy > 0 else 2)

    def is_relay(sy):
        return gy == (3 if sy > 0 else 0)

    def to_relay(n, sy):
        fy = HALO if sy < 0 else cy
        return pltpu.make_async_remote_copy(
            src_ref=wide_f.at[rows_apart[n] : rows_apart[n] + HALO, fy : fy + HALO],
            dst_ref=held.at[n - 2],
            send_sem=f_send.at[2 * n + (sy > 0)], recv_sem=relay_recv.at[n - 2],
            device_id=(gx, gy + 2 * sy), device_id_type=MESH,
        )

    def from_relay(n, sy):
        ty = cy + HALO if sy < 0 else 0
        return pltpu.make_async_remote_copy(
            src_ref=held.at[n - 2],
            dst_ref=wide_f.at[rows_apart[n] : rows_apart[n] + HALO, ty : ty + HALO],
            send_sem=relay_send.at[n - 2], recv_sem=f_recv.at[2 * n + (sy > 0)],
            device_id=(gx, gy - sy), device_id_type=MESH,
        )

    def pass_on(n):
        for sy in (-1, 1):
            @pl.when(is_relay(sy))
            def _():
                to_relay(n, sy).wait_recv()
                from_relay(n, sy).start()

    for n in relayed:
        for sy in (-1, 1):
            @pl.when(is_source(sy))
            def _():
                to_relay(n, sy).start()
    for n in range(len(rows_apart)):
        for sy in (-1, 1):
            direct = exists(0, sy)
            if n in relayed:
                direct = jnp.logical_and(direct, jnp.logical_not(is_source(sy)))

            @pl.when(direct)
            def _():
                chunk(n, sy).start()
        if n == 1:
            for sx in (-1, 1):
                @pl.when(exists(sx, 0))
                def _():
                    along_x(sx, 0).start()

    def take_chunk(n):
        for sy in (-1, 1):
            @pl.when(exists(0, -sy))
            def _():
                chunk(n, sy).wait_recv()
            for sx in (-1, 1):
                if n == (sx > 0):
                    @pl.when(exists(sx, -sy))
                    def _():
                        along_x(sx, sy).start()

    def take_x(sides):
        for sy in sides:
            for sx in (-1, 1):
                @pl.when(exists(-sx, -sy))
                def _():
                    along_x(sx, sy).wait_recv()

    def sent_f():
        for sy in (-1, 1):
            for n in range(len(rows_apart)):
                @pl.when(exists(0, sy))
                def _():
                    chunk(n, sy).wait_send()
                if n in relayed:
                    @pl.when(is_relay(sy))
                    def _():
                        from_relay(n, sy).wait_send()
        for sy in (0, -1, 1):
            for sx in (-1, 1):
                @pl.when(exists(sx, -sy))
                def _():
                    along_x(sx, sy).wait_send()

    for n, (nat, fwd, bwd) in enumerate(((wn1_ref, w1_ref, w1b_ref), (wn2_ref, w2_ref, w2b_ref))):
        local[2 + n].wait()
        wide = nat[...].astype(F32)
        for b in range(3):
            fwd[b * chans : (b + 1) * chans, :] = jnp.concatenate(
                [wide[a * 9 + b * 3 + c] for a in range(3) for c in range(3)], axis=1
            ).astype(BF)
        rows = wt.shape[0]
        wt[...] = jnp.zeros_like(wt)
        for a in range(3):
            for c in range(3):
                first = (a * 3 + c) * chans
                wt[first : first + chans, 0 : 3 * chans] = jnp.concatenate(
                    [wide[(2 - a) * 9 + (2 - b) * 3 + 2 - c] for b in range(3)], axis=1
                )
        turned = wt[...].T
        bwd[...] = turned[0 : 3 * chans, 0 : 9 * chans].astype(BF)

    half = depth // 2
    px, py = cx // 2, cy // 2
    spread = (
        lax.broadcasted_iota(jnp.int32, (half, depth), 1) // 2
        == lax.broadcasted_iota(jnp.int32, (half, depth), 0)
    ).astype(BF)
    local[6].wait()
    local[7].wait()
    for n, ref in enumerate((gp_ref, pc_ref)):
        for c in range(chans):
            for x in range(px):
                first = (c * px + x) * py
                pt[n, first : first + py, 0:half] = ref[c, x].astype(F32)
        if n:
            for side, y in enumerate((0, py - 1)):
                for x in range(0, px, 2):
                    pair = [pt[n, pl.ds((x + k) * py + y, chans, stride=px * py), :] for k in range(2)]
                    edge_k[side, x // 2] = jnp.concatenate(
                        [tile[:, 0:half] for tile in pair], axis=1
                    ).astype(BF)
        pt[n] = jnp.dot(pt[n, :, 0:half].astype(BF), spread, preferred_element_type=F32)

    def pooled(n, x, y):
        return pt[n, pl.ds(x * py + y, chans, stride=px * py), :]

    for x in range(px):
        for y in range(py):
            wide_k[x + 1, y + 1] = pooled(1, x, y).astype(BF)

    def choice_y(sy):
        side = int(sy > 0)
        return pltpu.make_async_remote_copy(
            src_ref=edge_k.at[side], dst_ref=land_k.at[side],
            send_sem=k_send.at[side], recv_sem=k_recv.at[side],
            device_id=(gx, gy + sy), device_id_type=MESH,
        )

    def choice_x(sx):
        side = int(sx > 0)
        return pltpu.make_async_remote_copy(
            src_ref=wide_k.at[px if sx > 0 else 1], dst_ref=wide_k.at[0 if sx > 0 else px + 1],
            send_sem=k_send.at[2 + side], recv_sem=k_recv.at[2 + side],
            device_id=(gx + sx, gy), device_id_type=MESH,
        )

    def choices_out():
        for sy in (-1, 1):
            @pl.when(exists(0, sy))
            def _():
                choice_y(sy).start()

    def choices_on():
        for sy in (-1, 1):
            @pl.when(exists(0, -sy))
            def _():
                choice_y(sy).wait_recv()
            twice = (
                lax.broadcasted_iota(jnp.int32, (depth, 2 * depth), 1) // 2
                == lax.broadcasted_iota(jnp.int32, (depth, 2 * depth), 0)
            ).astype(BF)
            for x in range(0, px, 2):
                both = jnp.dot(
                    land_k[int(sy > 0), x // 2], twice, preferred_element_type=F32
                ).astype(BF)
                for k in range(2):
                    wide_k[x + 1 + k, 0 if sy > 0 else py + 1] = both[:, lanes_of(k)]
        for sx in (-1, 1):
            @pl.when(exists(sx, 0))
            def _():
                choice_x(sx).start()

    def choices_in():
        for sx in (-1, 1):
            @pl.when(exists(-sx, 0))
            def _():
                choice_x(sx).wait_recv()

    def choices_sent():
        for side in (-1, 1):
            @pl.when(exists(0, side))
            def _():
                choice_y(side).wait_send()

            @pl.when(exists(side, 0))
            def _():
                choice_x(side).wait_send()

    same = lax.broadcasted_iota(jnp.int32, (chans, chans), 0) == lax.broadcasted_iota(
        jnp.int32, (chans, chans), 1
    )
    local[4].wait()
    local[5].wait()
    bias_one, bias_two = [
        jnp.sum(jnp.where(same, ref[...], 0.0), axis=1, keepdims=True) for ref in (b1_ref, b2_ref)
    ]
    lane = lax.broadcasted_iota(jnp.int32, (1, depth), 1)
    not_first = lane != 0
    not_last = lane != depth - 1
    lane_odd = lane % 2

    def flags(x, y):
        brick = gx * (cx // 8) + (x + 8 - HALO) // 8
        return mz_ref[brick, pl.ds(gy * (cy // 8) + (y + 8 - HALO) // 8, 1), :]

    def lanes_of(y, count=1):
        return slice(y * depth, (y + count) * depth)

    def put(stack, x, y, value):
        rounded = value.astype(BF)
        wide = rounded.astype(F32)
        where = lanes_of(y)
        stack[x, 0:chans, where] = jnp.where(not_first, pltpu.roll(wide, 1, 1), 0.0).astype(BF)
        stack[x, chans : 2 * chans, where] = rounded
        stack[x, 2 * chans : 3 * chans, where] = jnp.where(
            not_last, pltpu.roll(wide, depth - 1, 1), 0.0
        ).astype(BF)
        return rounded

    def put_cell(x, y):
        put(s1, x, y, jnp.where(flags(x, y) > 0, wide_f[x, y].astype(F32), 0.0))

    def conv(weight, stack, x, first, count, outs, total):
        rows = stack[pl.ds(x, 3), :, lanes_of(first, count)].reshape(9 * chans, count * depth)
        full = jnp.dot(weight[...], rows, preferred_element_type=F32)
        for t in range(count):
            for b in range(3):
                y = first + t - b
                if 0 <= y < outs:
                    piece = full[b * chans : (b + 1) * chans, lanes_of(t)]
                    total[y] = total[y] + piece if y in total else piece
        return total

    def grad(slot, delta, stack, x, first):
        width = (cy + 2) * depth
        rows = stack[pl.ds(x, 3), :, first * depth : first * depth + width].reshape(9 * chans, width)
        shifted = []
        for b in range(3):
            parts = []
            if b:
                parts.append(jnp.zeros((chans, b * depth), BF))
            parts.append(delta)
            if b < 2:
                parts.append(jnp.zeros((chans, (2 - b) * depth), BF))
            shifted.append(jnp.concatenate(parts, axis=1))
        left = jnp.concatenate(shifted, axis=0)
        right = jnp.concatenate([rows, jnp.ones((SPARE, width), BF)], axis=0)
        gw_ref[slot, :, 0 : 3 * chans] += lax.dot_general(
            right, left, (((1,), (1,)), ((), ())), preferred_element_type=F32
        )

    def pack(slot):
        total = gw_ref[slot]

        def block(n, b):
            return total[n * chans : (n + 1) * chans, b * chans : (b + 1) * chans]

        last = [block(n, b) for n in (7, 8) for b in range(3)]
        last.append(jnp.broadcast_to(total[9 * chans : 9 * chans + 1, 0:chans], (chans, chans)))
        full = jnp.concatenate(
            [
                jnp.concatenate([total[n * chans : (n + 1) * chans, 0 : 3 * chans], last[n]], axis=1)
                for n in range(7)
            ],
            axis=0,
        )
        gs[slot] = full.reshape(gs.shape[1:]).astype(BF)

    def sum_copies(slot, phase):
        if phase == 0:
            moves = [(gs.at[slot, 1 - core], r0.at[slot], partner)]
        elif phase == 1:
            moves = [(q1.at[slot, gy], q1.at[slot, gy], peer_y(k)) for k in range(1, ny)]
        elif phase == 2:
            moves = [(q2.at[slot, gz], q2.at[slot, gz], peer_z(k)) for k in range(1, nz)]
        else:
            moves = [(tot.at[slot, core], tot.at[slot, core], partner)]
        return [
            pltpu.make_async_remote_copy(
                src_ref=src, dst_ref=dst,
                send_sem=sum_send.at[slot, phase, k], recv_sem=sum_recv.at[slot, phase, k],
                device_id=device, device_id_type=MESH,
            )
            for k, (src, dst, device) in enumerate(moves)
        ]

    def sum_start(slot, phase):
        for copy in sum_copies(slot, phase):
            copy.start()

    def sum_finish(slot, phase):
        for copy in sum_copies(slot, phase):
            copy.wait_recv()
        if phase == 0:
            q1[slot, gy] = (gs[slot, core].astype(F32) + r0[slot].astype(F32)).astype(BF)
        if phase == 1:
            q2[slot, gz] = sum(q1[slot, k].astype(F32) for k in range(ny)).astype(BF)
        if phase == 2:
            tot[slot, core] = sum(q2[slot, k].astype(F32) for k in range(nz)).astype(BF)

    for x in range(cx):
        for y in range(cy):
            put_cell(x + HALO, y + HALO)

    def early_one(x):
        total = conv(w1_ref, s1, x, HALO, cy, cy + 2, {})
        for y in range(2, cy):
            hide(x, y, total[y])
        for n, y in enumerate((0, 1, cy, cy + 1)):
            part1[x, n] = total[y]

    def hide(x, y, pre):
        mask = flags(x + 1, y + 1)
        put(s2, x, y, jnp.where(mask > 0, jnp.maximum(pre + bias_one, 0.0), 0.0))

    for x in range(2, cx):
        early_one(x)
    for n in relayed[:1]:
        pass_on(n)
    take_x((0,))
    for n in relayed[1:]:
        pass_on(n)
    choices_out()
    for n in (0, 1, cx + 2, cx + 3):
        for y in range(cy):
            put_cell(n, y + HALO)
    for x in (0, 1, cx, cx + 1):
        early_one(x)

    def early_two(x):
        total = conv(w2_ref, s2, x, 2, cy - 2, cy, {})
        for y in range(cy):
            part2[x, y] = total[y]

    for x in range(cx):
        early_two(x)

    edges = (0, 1, cy, cy + 1)

    def late_one(x):
        total = {y: part1[x, n] for n, y in enumerate(edges)}
        conv(w1_ref, s1, x, 0, 2, cy + 2, total)
        conv(w1_ref, s1, x, cy + 2, 2, cy + 2, total)
        for y in edges:
            hide(x, y, total[y])

    def put_rows(x):
        for n in range(x, x + HALO):
            for y in (0, 1, cy + 2, cy + 3):
                put_cell(n, y)

    def choose(x):
        total = {y: part2[x, y] for y in range(cy)}
        conv(w2_ref, s2, x, 0, 2, cy, total)
        conv(w2_ref, s2, x, cy, 2, cy, total)
        out = []
        for y in range(cy):
            mask = flags(x + HALO, y + HALO)
            code = (4 * (x % 2) + 2 * (y % 2) + lane_odd).astype(F32)
            hit = jnp.where(pooled(1, x // 2, y // 2) == code, mask, 0.0)
            chosen = jnp.where(total[y] + bias_two > 0, hit, 0.0)
            delta = jnp.where(chosen > 0, pooled(0, x // 2, y // 2), 0.0)
            put(s3, x + HALO, y + HALO, delta)
            out.append(delta)
        return out

    def choose_pair(x):
        rows = [choose(2 * x), choose(2 * x + 1)]
        for y in range(py):
            cells = [row[2 * y + k] for row in rows for k in range(2)]
            wide_w[x + 1, y + 1] = sum(cells).astype(BF)

    ready = 2
    for n, x in enumerate(rows_apart):
        take_chunk(n)
        if n == 1:
            put_rows(rows_apart[0])
        if n:
            put_rows(x)
        if n == len(rows_apart) - 1:
            choices_on()
        if n > 1:
            last_row = cx if n == len(rows_apart) - 1 else x
            for row in range(ready, last_row):
                late_one(row)
            ready = last_row
    for x in range(1, px - 1):
        choose_pair(x)
    send(True)
    take_x((-1, 1))
    for x in (0, cx + HALO):
        put_rows(x)
    for x in (0, 1, cx, cx + 1):
        late_one(x)
    for x in (0, px - 1):
        choose_pair(x)

    send(False)

    for x in range(cx):
        delta = s3[x + HALO, chans : 2 * chans, HALO * depth : (HALO + cy) * depth]
        grad(1, delta, s2, x, 0)

    pack(1)
    sum_start(1, 0)

    def put_delta(x, y):
        code = (4 * (x % 2) + 2 * (y % 2) + lane_odd).astype(F32)
        hit = wide_k[x // 2, y // 2].astype(F32) == code
        value = jnp.where(hit, wide_w[x // 2, y // 2].astype(F32), 0.0)
        put(s3, x, y, jnp.where(flags(x, y) > 0, value, 0.0))

    def put_back(x, y, total):
        hidden = s2[x, chans : 2 * chans, lanes_of(y)].astype(F32)
        put(s4, x, y, jnp.where(hidden > 0, total, 0.0))

    def early_back(x):
        total = conv(w2b_ref, s3, x, HALO, cy, cy + 2, {})
        for y in range(2, cy):
            put_back(x, y, total[y])
        for n, y in enumerate(edges):
            part1[x, n] = total[y]

    def late_back(x):
        total = {y: part1[x, n] for n, y in enumerate(edges)}
        conv(w2b_ref, s3, x, 0, 2, cy + 2, total)
        conv(w2b_ref, s3, x, cy + 2, 2, cy + 2, total)
        for y in edges:
            put_back(x, y, total[y])

    def back(x):
        total = conv(w2b_ref, s3, x, 0, cy + 4, cy + 2, {})
        for y in range(cy + 2):
            put_back(x, y, total[y])

    for x in range(2, cx):
        early_back(x)

    sum_finish(1, 0)
    sum_start(1, 1)
    choices_in()
    arrive()
    for x in range(cx + 2 * HALO):
        inner = HALO <= x < cx + HALO
        for y in (0, 1, cy + 2, cy + 3) if inner else range(cy + 2 * HALO):
            put_delta(x, y)
    for x in range(2, cx):
        late_back(x)
    for x in (0, 1, cx, cx + 1):
        back(x)

    for x in range(cx):
        delta = s4[x + 1, chans : 2 * chans, depth : (1 + cy) * depth]
        grad(0, delta, s1, x + 1, 1)

    pack(0)
    sum_start(0, 0)
    sum_finish(1, 1)
    sum_start(1, 2)

    def last(x):
        total = conv(w1b_ref, s4, x, 0, cy + 2, cy, {})
        for y in range(cy):
            mask = flags(x + HALO, y + HALO)
            go[cell_rows(x, y), :] = jnp.where(mask > 0, total[y], 0.0)

    for x in range(cx):
        if x == cx // 2:
            sum_finish(0, 0)
            sum_start(0, 1)
        last(x)
    gin_ref[...] = go[...].reshape(chans, cx, cy, depth).astype(BF)

    sum_finish(0, 1)
    sum_start(0, 2)
    sum_finish(1, 2)
    sum_start(1, 3)
    sum_finish(0, 2)
    sum_start(0, 3)
    sum_finish(1, 3)
    sum_finish(0, 3)

    sent_f()
    choices_sent()
    sent()
    for slot in range(2):
        for phase in range(4):
            for copy in sum_copies(slot, phase):
                copy.wait_send()


def publish_kernel(scale, chans, gin_ref, tot, gin_hbm, gw1, gb1, gw2, gb2, out, bias, sem):
    copies = [pltpu.make_async_copy(gin_ref, gin_hbm, sem.at[0])]
    copies[0].start()
    for slot, (weight_out, bias_out) in enumerate(((gw1, gb1), (gw2, gb2))):
        full = jnp.concatenate([tot[slot, 0], tot[slot, 1]], axis=0).astype(F32) * scale
        turned = jnp.concatenate([full, jnp.zeros((chans, full.shape[1]), F32)], axis=0).T
        for a in range(3):
            for b in range(3):
                for c in range(3):
                    n = a * 3 + c
                    row, column = (b, n) if n < 7 else (3, (n - 7) * 3 + b)
                    out[slot, a * 9 + b * 3 + c] = turned[
                        row * chans : (row + 1) * chans, column * chans : (column + 1) * chans
                    ]
        bias[slot] = full[6 * chans : 6 * chans + 1, 3 * chans : 4 * chans]
        for src, dst in ((out.at[slot], weight_out), (bias.at[slot], bias_out)):
            copies.append(pltpu.make_async_copy(src, dst, sem.at[len(copies)]))
            copies[-1].start()
    for copy in copies:
        copy.wait()


def body(features, occupancy, weight_one, bias_one, weight_two, bias_two, grad_pooled, pool_choice):
    chans, cx, cy, depth = features.shape
    nx, ny = lax.axis_size("gx"), lax.axis_size("gy")
    nz = nx // 2
    part = 7 * chans // 2
    bx, by, bz = occupancy.shape
    lanes = -(-(9 * chans + 1) // 128) * 128

    def taps_first(weight):
        return weight.transpose(1, 2, 3, 0, 4).reshape(27, chans, chans)

    def vm(shape, dtype):
        return pltpu.VMEM(shape, dtype)

    px, py, half = grad_pooled.shape[1:]
    hbm = pl.BlockSpec(memory_space=pltpu.HBM)
    vmem = pl.BlockSpec(memory_space=pltpu.VMEM)
    gin, tot = pl.pallas_call(
        functools.partial(main_kernel, nx, ny, cx, cy, depth, chans),
        out_shape=(
            jax.ShapeDtypeStruct(features.shape, BF),
            jax.ShapeDtypeStruct((2, 2, part, 4 * chans), BF),
        ),
        in_specs=[hbm] * 8,
        out_specs=(vmem,) * 2,
        scratch_shapes=[
            vm(features.shape, BF),
            vm(occupancy.shape, jnp.int32),
            vm((27, chans, chans), BF),
            vm((27, chans, chans), BF),
            vm((1, chans), F32),
            vm((1, chans), F32),
            vm(grad_pooled.shape, BF),
            vm(pool_choice.shape, jnp.int32),
            vm((chans * cx * cy, depth), F32),
            vm((chans * cx * cy, depth), F32),
            vm((2, chans * px * py, depth), F32),
            vm((lanes, 128), F32),
            vm((bx + 2, by + 2, depth), F32),
            vm((3 * chans, 9 * chans), BF),
            vm((3 * chans, 9 * chans), BF),
            vm((3 * chans, 9 * chans), BF),
            vm((3 * chans, 9 * chans), BF),
            vm((cx + 4, cy + 4, chans, depth), BF),
            vm((px + 2, py + 2, chans, depth), BF),
            vm((px + 2, py + 2, chans, depth), BF),
            vm((cx + 2, 4, chans, depth), F32),
            vm((cx, cy, chans, depth), F32),
            vm((cx + 4, 3 * chans, (cy + 4) * depth), BF),
            vm((cx + 2, 3 * chans, (cy + 2) * depth), BF),
            vm((cx + 4, 3 * chans, (cy + 4) * depth), BF),
            vm((cx + 2, 3 * chans, (cy + 2) * depth), BF),
            vm((2, 9 * chans + SPARE, 4 * chans), F32),
            vm((2, 2, part, 4 * chans), BF),
            vm((2, part, 4 * chans), BF),
            vm((2, ny, part, 4 * chans), BF),
            vm((2, nz, part, 4 * chans), BF),
            vm((cx // HALO - 2, HALO, HALO, chans, depth), BF),
            vm((2, px // 2, chans, depth), BF),
            vm((2, px // 2, chans, depth), BF),
            pltpu.SemaphoreType.DMA((4,)),
            pltpu.SemaphoreType.DMA((4,)),
            pltpu.SemaphoreType.DMA((8,)),
            pltpu.SemaphoreType.DMA((2 * (cx // HALO) + 6,)),
            pltpu.SemaphoreType.DMA((2 * (cx // HALO) + 6,)),
            pltpu.SemaphoreType.DMA((cx // HALO - 2,)),
            pltpu.SemaphoreType.DMA((cx // HALO - 2,)),
            pltpu.SemaphoreType.DMA((12,)),
            pltpu.SemaphoreType.DMA((12,)),
            pltpu.SemaphoreType.DMA((2, 4, max(ny, nz))),
            pltpu.SemaphoreType.DMA((2, 4, max(ny, nz))),
        ],
        compiler_params=pltpu.CompilerParams(
            collective_id=0, has_side_effects=True, vmem_limit_bytes=48 * 2**20
        ),
        name="main",
    )(*[pltpu.with_memory_space_constraint(v, pltpu.HBM) for v in (
        features, occupancy, taps_first(weight_one), taps_first(weight_two),
        bias_one.reshape(1, chans), bias_two.reshape(1, chans), grad_pooled, pool_choice,
    )])

    scale = 1.0 / math.sqrt(cx * nx * cy * ny * depth)
    taps = jax.ShapeDtypeStruct((27, chans, chans), F32)
    row = jax.ShapeDtypeStruct((1, chans), F32)
    gin, gw1, gb1, gw2, gb2 = pl.pallas_call(
        functools.partial(publish_kernel, scale, chans),
        out_shape=(jax.ShapeDtypeStruct(features.shape, BF), taps, row, taps, row),
        in_specs=[vmem] * 2,
        out_specs=(hbm,) * 5,
        scratch_shapes=[
            vm((2, 27, chans, chans), F32),
            vm((2, 1, chans), F32),
            pltpu.SemaphoreType.DMA((5,)),
        ],
        compiler_params=pltpu.CompilerParams(vmem_limit_bytes=8 * 2**20),
        name="publish",
    )(gin, tot)

    def taps_back(grads):
        return grads.reshape(3, 3, 3, chans, chans).transpose(3, 0, 1, 2, 4)

    return gin, taps_back(gw1), gb1.reshape(chans), taps_back(gw2), gb2.reshape(chans)


def solution(mesh):
    spread = P(None, "gx", "gy", None)
    return jax.shard_map(
        body,
        mesh=mesh,
        in_specs=(spread, P(), P(), P(), P(), P(), spread, spread),
        out_specs=(spread, P(), P(), P(), P()),
        check_vma=False,
    )
```
